256 devices in a mesh: ctx: 64 (over z, x, core), head: 4 (over y).
Axes of the slice: x: 4, y: 4, z: 8, core: 2. Of those that a mesh axis runs over, the one named last changes fastest.
Arguments:
- queries: bfloat16 [8192, 6144], P('ctx', 'head'), may hold values from -0.75 to 0.75
- keys: bfloat16 [8192, 6144], P('ctx', 'head'), may hold values from -0.75 to 0.75
- values: bfloat16 [8192, 6144], P('ctx', 'head'), may hold values from -1.2 to 1.2
- normed_grad: bfloat16 [8192, 6144], P('ctx', 'head'), may hold values from -1.5 to 1.5
- gain: bfloat16 [6144], P('head'), may hold values from 0.5 to 1.5
- segment: int32 [8192], P('ctx'), may hold values from 0 to 15, never falling along the last dimension, each value on 1 to 2048 neighbouring positions
- plan: int32 [8192], replicated, may hold values from 0 to 8191, as said below
Outputs:
- normed: bfloat16 [8192, 6144], P('ctx', 'head')
- query_grad: bfloat16 [8192, 6144], P('ctx', 'head')
- key_grad: bfloat16 [8192, 6144], P('ctx', 'head')
- value_grad: bfloat16 [8192, 6144], P('ctx', 'head')
The draws below stay inside these ranges and needn't reach their ends.
Inputs may be any that keep to these rules, and one draw needn't show every extreme that they name: `plan`: A permutation. Loader rows come in aligned blocks of 2 rows that stay together and in order, and the rows held by one index of ctx send exactly one such block to each index of ctx.
All inputs are finite; a program needn't handle non-finite values.
Results may differ from the reference program's by a relative error of at most 0.012.
Values may be sent and summed in bfloat16 or wider, within the bound.
A program may use at most 128 MiB of HBM per device.

```python
import math
import jax
import jax.numpy as jnp
import numpy as np
from jax import lax

HEADS = 48
HEAD_DIM = 128
TOK_DEV = 128
TOKENS = 8192
UNIT = 2
PATIENTS = 16
LONGEST = 2048


def draw_values(key, part):
    scale_key, entry_key = jax.random.split(key)
    low_end, high_end = (0.06, 0.25)
    log_scales = jax.random.uniform(scale_key, (HEADS,), jnp.float32, math.log(low_end), math.log(high_end))
    head_scale = jnp.sort(jnp.exp(log_scales))
    entries = jax.random.truncated_normal(entry_key, -4.0, 4.0, (TOKENS, HEADS, HEAD_DIM), jnp.float32)
    return (entries * head_scale[None, :, None]).reshape(TOKENS, HEADS * HEAD_DIM).astype(jnp.bfloat16)


def draw_plan(key, part):
    devices_n = TOKENS // TOK_DEV
    send_key, slot_key = jax.random.split(key)
    offsets = jax.vmap(lambda subkey: jax.random.permutation(subkey, devices_n))(jax.random.split(send_key, devices_n))
    sources = jnp.arange(devices_n, dtype=jnp.int32)[:, None]
    targets = (sources + offsets.astype(jnp.int32)) % devices_n
    orders = jax.vmap(lambda subkey: jax.random.permutation(subkey, devices_n))(jax.random.split(slot_key, devices_n)).astype(jnp.int32)
    places = orders[targets, jnp.broadcast_to(sources, targets.shape)]
    starts = (targets * devices_n + places) * UNIT
    rows_all = starts[:, :, None] + jnp.arange(UNIT, dtype=jnp.int32)[None, None, :]
    return rows_all.reshape(TOKENS).astype(jnp.int32)


def level_of(stream_key, shape, shards, smallest, largest):
    level, own = 1.0, jax.random.fold_in(stream_key, 6)
    for dim, blocks in shards:
        steps = jnp.exp(jax.random.uniform(jax.random.fold_in(own, dim), (blocks,), jnp.float32, smallest / len(shards), largest / len(shards)))
        level = level * jnp.repeat(steps, shape[dim] // blocks).reshape([-1 if axis == dim else 1 for axis in range(len(shape))])
    return level


def split_up(count, total, most, skew):
    portions = [(1 << 20) // math.isqrt(grade ** skew) + 1 for grade in range(2, count + 1)]
    surplus, counts = total - most - (count - 1), [1] * (count - 1)
    while surplus > 0:
        free = [i for i in range(count - 1) if counts[i] < most]
        pool, remaining = sum([portions[i] for i in free]), surplus
        for i in free:
            addition = min(most - counts[i], max(1, remaining * portions[i] // pool), surplus)
            counts[i] = counts[i] + addition
            surplus = surplus - addition
    return np.array([most] + counts)


def ragged(rng, number_of, total, limit, slope):
    if number_of == 2:
        one = jax.random.randint(rng, (), max(1, total - limit), min(limit, total - 1) + 1)
        return jnp.stack([one, total - one])
    sizes = jnp.asarray(split_up(number_of, total, limit, slope), jnp.int32)
    pairs = (number_of - 1) // 2
    donor, receiver = sizes[1:1 + 2 * pairs:2], sizes[2:2 + 2 * pairs:2]
    margin = jnp.minimum(donor - 1, limit - receiver)
    shifted = jax.random.randint(jax.random.fold_in(rng, 1), (pairs,), 0, 1 << 20) % (margin + 1)
    sizes = sizes.at[1:1 + 2 * pairs:2].set(donor - shifted).at[2:2 + 2 * pairs:2].set(receiver + shifted)
    return sizes[jax.random.permutation(jax.random.fold_in(rng, 2), number_of)]


def centred(stream_key, dims, deviation, bound, cuts=(), kind=jnp.bfloat16):
    values = jax.random.normal(stream_key, dims, jnp.float32) * deviation
    if len(cuts) > 0:
        values = level_of(stream_key, dims, cuts, -0.22, 0.18) * values
    return jnp.clip(values, min=-bound, max=bound).astype(kind)


def setup_inputs(seed: int = 0) -> dict:
    seeds = jax.random.split(jax.random.key(seed), 8)
    queries = centred(seeds[0], (TOKENS, HEADS * HEAD_DIM), 0.125, 0.75, ((0, 64), (1, 4)))
    keys = centred(seeds[1], (TOKENS, HEADS * HEAD_DIM), 0.125, 0.75, ((0, 64), (1, 4)))
    values = draw_values(jax.random.fold_in(seeds[7], 71), 0)
    normed_grad = centred(seeds[3], (TOKENS, HEADS * HEAD_DIM), 0.25, 1.5, ((0, 64), (1, 4)))
    gain = jnp.clip(1.0 + 0.1 * jax.random.normal(seeds[4], (HEADS * HEAD_DIM,), jnp.float32), 0.5, 1.5).astype(jnp.bfloat16)
    segment = jnp.searchsorted(jnp.cumsum(ragged(seeds[5], PATIENTS, TOKENS, LONGEST, 1)), jnp.arange(TOKENS), side="right").astype(jnp.int32)
    plan = draw_plan(jax.random.fold_in(seeds[7], 71), 0)
    return dict(queries=queries, keys=keys, values=values, normed_grad=normed_grad, gain=gain, segment=segment, plan=plan)


def upcast(source_rows):
    return source_rows.astype(jnp.float32)

def reference(queries, keys, values, normed_grad, gain, segment, plan):
    block_rows = TOK_DEV
    block_count = TOKENS // TOK_DEV
    total_width = HEADS * HEAD_DIM
    source_of = jnp.zeros((TOKENS,), jnp.int32).at[plan].set(jnp.arange(TOKENS, dtype=jnp.int32))

    def arrange(source_rows):
        return jnp.take(source_rows, source_of, axis=0).reshape(block_count, block_rows, HEADS, HEAD_DIM)
    query_blocks = arrange(queries)
    key_blocks = arrange(keys)
    value_blocks = arrange(values)
    segment_blocks = segment.reshape(block_count, block_rows)
    positions = jnp.arange(block_rows, dtype=jnp.int32)
    zero_state = jnp.zeros((HEADS, HEAD_DIM, HEAD_DIM), jnp.float32)
    start_id = jnp.array(-1, jnp.int32)

    def visible_of(seg_row):
        return (positions[:, None] >= positions[None, :]) & (seg_row[:, None] == seg_row[None, :])

    def forward_step(carried, members):
        last_seen, carry_state = carried
        key_block, value_block, seg_row = members
        tail_rows = (seg_row == seg_row[-1])[:, None, None]
        local_state = jnp.einsum('ihd,ihe->hde', jnp.where(tail_rows, upcast(key_block), 0.0), upcast(value_block))
        carries = ((seg_row[0] == seg_row[-1]) & (seg_row[0] == last_seen)).astype(jnp.float32)
        return ((seg_row[-1], local_state + carries * carry_state), (last_seen, carry_state))
    _, (fwd_ids, fwd_states) = lax.scan(forward_step, (start_id, zero_state), (key_blocks, value_blocks, segment_blocks))

    def block_weights(query_block, key_block, seg_row):
        scores = jnp.einsum('ihd,jhd->hij', upcast(query_block), upcast(key_block))
        return jnp.where(visible_of(seg_row)[None], scores, 0.0).astype(jnp.bfloat16)

    def attend(members):
        query_block, key_block, value_block, seg_row, last_seen, carry_state = members
        weights_b = block_weights(query_block, key_block, seg_row)
        resume = (seg_row == last_seen).astype(jnp.float32)[:, None, None]
        carried_in = upcast(carry_state.astype(jnp.bfloat16))
        attended = jnp.einsum('hij,jhe->ihe', upcast(weights_b), upcast(value_block))
        attended = attended + resume * jnp.einsum('ihd,hde->ihe', upcast(query_block), carried_in)
        return attended.astype(jnp.bfloat16)
    attended = lax.map(attend, (query_blocks, key_blocks, value_blocks, segment_blocks, fwd_ids, fwd_states))
    attn_f = upcast(attended.reshape(TOKENS, total_width))
    inverse = lax.rsqrt(lax.optimization_barrier(jnp.mean(attn_f * attn_f, axis=1)) + 1e-05)
    normal_part = attn_f * inverse[:, None]
    gain_f = upcast(gain)
    normed = (normal_part * gain_f).astype(jnp.bfloat16)
    scaled_grad = upcast(normed_grad) * gain_f
    projection = lax.optimization_barrier(jnp.mean(scaled_grad * normal_part, axis=1))
    attn_grad = (inverse[:, None] * (scaled_grad - normal_part * projection[:, None])).astype(jnp.bfloat16)
    grad_blocks = attn_grad.reshape(block_count, block_rows, HEADS, HEAD_DIM)

    def backward_step(carried, members):
        first_seen, carry_state = carried
        query_block, grad_block, seg_row = members
        head_rows = (seg_row == seg_row[0])[:, None, None]
        local_state = jnp.einsum('ihd,ihe->hde', jnp.where(head_rows, upcast(query_block), 0.0), upcast(grad_block))
        carries = ((seg_row[0] == seg_row[-1]) & (seg_row[-1] == first_seen)).astype(jnp.float32)
        return ((seg_row[0], local_state + carries * carry_state), (first_seen, carry_state))
    _, (bwd_ids, bwd_states) = lax.scan(backward_step, (start_id, zero_state), (query_blocks, grad_blocks, segment_blocks), reverse=True)

    def differentiate(members):
        query_block, key_block, value_block, grad_block, seg_row, last_seen, carry_state, first_seen, back_state = members
        weights_b = block_weights(query_block, key_block, seg_row)
        grad_scores = jnp.einsum('ihe,jhe->hij', upcast(grad_block), upcast(value_block))
        grad_weights = jnp.where(visible_of(seg_row)[None], grad_scores, 0.0).astype(jnp.bfloat16)
        resume = (seg_row == last_seen).astype(jnp.float32)[:, None, None]
        reaches = (seg_row == first_seen).astype(jnp.float32)[:, None, None]
        carried_in = upcast(carry_state.astype(jnp.bfloat16))
        carried_back = upcast(back_state.astype(jnp.bfloat16))
        query_grad = jnp.einsum('hij,jhd->ihd', upcast(grad_weights), upcast(key_block))
        query_grad = query_grad + resume * jnp.einsum('ihe,hde->ihd', upcast(grad_block), carried_in)
        key_grad = jnp.einsum('hij,ihd->jhd', upcast(grad_weights), upcast(query_block))
        key_grad = key_grad + reaches * jnp.einsum('jhe,hde->jhd', upcast(value_block), carried_back)
        value_grad = jnp.einsum('hij,ihe->jhe', upcast(weights_b), upcast(grad_block))
        value_grad = value_grad + reaches * jnp.einsum('jhd,hde->jhe', upcast(key_block), carried_back)
        return (query_grad.astype(jnp.bfloat16), key_grad.astype(jnp.bfloat16), value_grad.astype(jnp.bfloat16))
    query_grad, key_grad, value_grad = lax.map(differentiate, (query_blocks, key_blocks, value_blocks, grad_blocks, segment_blocks, fwd_ids, fwd_states, bwd_ids, bwd_states))
    return (normed, query_grad.reshape(TOKENS, total_width), key_grad.reshape(TOKENS, total_width), value_grad.reshape(TOKENS, total_width))
```

```python
import jax
import jax.numpy as jnp
from jax import lax
from jax.experimental import pallas as pl
from jax.experimental.pallas import tpu as pltpu
from jax.sharding import PartitionSpec as P

HEADS = 48
HEAD_DIM = 128
ROWS = 128
LINES = 8
GROUP = 8
OWN_HEADS = 12
CHUNKS = 3
CHUNK_HEADS = OWN_HEADS // CHUNKS
WIDE = CHUNK_HEADS * HEAD_DIM
PARCELS = 3 * CHUNKS
BAND = ROWS // LINES
SLICE = WIDE // GROUP
HEAD_PEERS = 4
MESH = pl.DeviceIdType.MESH
F32 = jnp.float32
BF16 = jnp.bfloat16
Z_ORDER = (4, 3, 5, 2, 6, 1, 7)
G_ORDER = (4, 3, 5, 2, 6, 1, 7)


def nn(a, b):
    return lax.dot_general(a, b, (((1,), (0,)), ((), ())), preferred_element_type=F32)


def nt(a, b):
    return lax.dot_general(a, b, (((1,), (1,)), ((), ())), preferred_element_type=F32)


def tn(a, b):
    return lax.dot_general(a, b, (((0,), (0,)), ((), ())), preferred_element_type=F32)


def iota(dim):
    return lax.broadcasted_iota(jnp.int32, (ROWS, ROWS), dim)


def kernel(
    q_hbm, k_hbm, v_hbm, ng_hbm, gain_hbm, seg_hbm, plan_hbm,
    normed_hbm, qg_hbm, kg_hbm, vg_hbm,
    x, a, b, c, d, seq, ng, gain, seg, plan,
    seg_line, seg_all, mid, settle, vis, vist, tails, heads, resume, reaches,
    sf, srf, rf, zrf, csf, crf, sb, srb, rb, zrb, csb, crb,
    att, gr, wt, gwt, sq_send, sq_recv, kg_part, vg_part, o_n, o_q, o_k, o_v,
    load_sem, out_sem, seg_sem, send_sem, recv_sem,
):
    me = lax.axis_index("ctx")
    y = lax.axis_index("head")
    z = lax.div(me, GROUP)
    g = lax.rem(me, GROUP)

    def z_peer(dz):
        return lax.rem(z + dz, LINES)

    def g_peer(dg):
        return lax.rem(g + dg, GROUP)

    def ctx_of(zz, gg):
        return zz * GROUP + gg

    def band(i):
        return pl.ds(pl.multiple_of(i * BAND, BAND), BAND)

    def send(src, dst, stage, slot, ctx_to, head_to):
        pltpu.make_async_remote_copy(
            src_ref=src, dst_ref=dst, send_sem=send_sem.at[stage], recv_sem=recv_sem.at[slot],
            device_id=(ctx_to, head_to), device_id_type=MESH,
        ).start()

    def took(ref, slot):
        pltpu.make_async_copy(ref, ref, recv_sem.at[slot]).wait()

    order = []
    for j in range(CHUNKS):
        order.append((k_hbm, j))
        order.append((v_hbm, j))
    for j in range(CHUNKS):
        order.append((q_hbm, j))
    small = [
        pltpu.make_async_copy(plan_hbm, plan, load_sem.at[PARCELS]),
        pltpu.make_async_copy(seg_hbm, seg, load_sem.at[PARCELS + 1]),
        pltpu.make_async_copy(gain_hbm, gain, load_sem.at[PARCELS + 2]),
    ]
    for copy in small:
        copy.start()
    loads = []
    for p, (ref, j) in enumerate(order):
        copy = pltpu.make_async_copy(ref.at[:, WIDE * j : WIDE * (j + 1)], x.at[p], load_sem.at[p])
        copy.start()
        loads.append(copy)
    ng_copy = pltpu.make_async_copy(ng_hbm, ng, load_sem.at[PARCELS + 3])
    ng_copy.start()

    barrier = pltpu.get_barrier_semaphore()
    for dz in Z_ORDER:
        pl.semaphore_signal(barrier, inc=1, device_id=(ctx_of(z_peer(dz), g), y), device_id_type=MESH)
    for dg in G_ORDER:
        pl.semaphore_signal(barrier, inc=1, device_id=(ctx_of(z, g_peer(dg)), y), device_id_type=MESH)
    for dy in range(1, HEAD_PEERS):
        pl.semaphore_signal(
            barrier, inc=1, device_id=(me, lax.rem(y + dy, HEAD_PEERS)), device_id_type=MESH
        )

    for copy in small:
        copy.wait()
    rows_i = iota(0)
    cols_i = iota(1)
    own_plan = plan[pl.ds(me, 1), :]
    slot_of = 2 * lax.shift_right_logical(own_plan, 7) + (cols_i[0:1, :] & 1)
    leave = (rows_i == slot_of).astype(F32).astype(BF16)
    for p in range(PARCELS):
        loads[p].wait()
        a[p] = nn(leave, x[p]).astype(BF16)

    seg_row = seg[...]
    seg_f = seg_row.astype(F32)
    seg_lanes = jnp.broadcast_to(seg_f, (ROWS, ROWS))
    seg_rows = seg_lanes.T
    last_here = jnp.broadcast_to(seg_f[:, ROWS - 1 : ROWS], (1, ROWS))
    first_here = jnp.broadcast_to(seg_f[:, 0:1], (1, ROWS))
    same = seg_lanes == seg_rows
    vis[...] = jnp.where(same & (rows_i >= cols_i), 1.0, 0.0)
    vist[...] = jnp.where(same & (cols_i >= rows_i), 1.0, 0.0)
    tails[...] = jnp.where(seg_rows == last_here, 1.0, 0.0).astype(BF16)
    heads[...] = jnp.where(seg_rows == first_here, 1.0, 0.0).astype(BF16)
    seg_line[z, 0:1, :] = last_here
    seg_line[z, 1:2, :] = first_here

    pl.semaphore_wait(barrier, LINES - 1 + GROUP - 1 + HEAD_PEERS - 1)

    for dz in Z_ORDER:
        send(seg_line.at[z], seg_line.at[z], 0, 0, ctx_of(z_peer(dz), g), y)
    for p in range(PARCELS):
        for dz in Z_ORDER:
            zt = z_peer(dz)
            send(a.at[p, band(zt)], b.at[p, band(z)], 1, 2 + p, ctx_of(zt, g), y)
        b[p, band(z), :] = a[p, band(z), :]

    source = ((rows_i & 15) >> 1) * BAND + (rows_i >> 4) * 2 + (rows_i & 1)
    mid[...] = (cols_i == source).astype(F32).astype(BF16)
    plan_all = plan[...]
    lanes = lax.broadcasted_iota(jnp.int32, (LINES * GROUP, ROWS), 1)
    mine = (lax.shift_right_logical(plan_all, 7) == me) & ((lanes & 1) == 0)
    start = jnp.sum(jnp.where(mine, (plan_all & 127).astype(F32), 0.0), axis=1, keepdims=True)
    start = jnp.broadcast_to(start, (LINES * GROUP, ROWS)).astype(BF16)
    pick_rows = lax.broadcasted_iota(jnp.int32, (ROWS, LINES * GROUP), 0)
    pick_cols = lax.broadcasted_iota(jnp.int32, (ROWS, LINES * GROUP), 1)
    pick = (pick_cols == ((pick_rows & 15) >> 1) * GROUP + (pick_rows >> 4)).astype(F32).astype(BF16)
    place = nn(pick, start) + (rows_i & 1).astype(F32)
    settle[...] = jnp.where(cols_i.astype(F32) == place, 1.0, 0.0).T.astype(BF16)

    def first_hop(p):
        took(b.at[p, 0 : ROWS - BAND], 2 + p)
        c[p] = nn(mid[...], b[p]).astype(BF16)
        for dg in G_ORDER:
            gt = g_peer(dg)
            send(c.at[p, band(gt)], d.at[p, band(g)], 2, 2 + PARCELS + p, ctx_of(z, gt), y)
        d[p, band(g), :] = c[p, band(g), :]

    def second_hop(p):
        took(d.at[p, 0 : ROWS - BAND], 2 + PARCELS + p)
        seq[p] = nn(settle[...], d[p]).astype(BF16)

    def lanes_of(hh):
        return slice(HEAD_DIM * hh, HEAD_DIM * (hh + 1))

    def k_of(j, hh):
        return seq[2 * j, :, lanes_of(hh)]

    def v_of(j, hh):
        return seq[2 * j + 1, :, lanes_of(hh)]

    def q_of(j, hh):
        return seq[2 * CHUNKS + j, :, lanes_of(hh)]

    state_slot = 2 + 2 * PARCELS

    def spread(j, local, landed, stage, slot):
        for dg in G_ORDER:
            gt = g_peer(dg)
            send(local.at[j, gt], landed.at[j, g], stage, slot, ctx_of(z, gt), y)
        landed[j, g] = local[j, g]

    def forward_state(j):
        for hh in range(CHUNK_HEADS):
            state = tn(k_of(j, hh) * tails[...], v_of(j, hh)).astype(BF16)
            sf[j, 2 * hh : 2 * hh + 2] = state.reshape(2, SLICE, HEAD_DIM)
        spread(j, sf, srf, 3, state_slot + j)

    def backward_state(j):
        for hh in range(CHUNK_HEADS):
            state = tn(q_of(j, hh) * heads[...], gr[j, :, lanes_of(hh)]).astype(BF16)
            sb[j, 2 * hh : 2 * hh + 2] = state.reshape(2, SLICE, HEAD_DIM)
        spread(j, sb, srb, 6, state_slot + 3 * CHUNKS + j)

    def last_of(zz, gg):
        return seg_all[gg, zz, 0:1, :]

    def first_of(zz, gg):
        return seg_all[gg, zz, 1:2, :]

    def flag(one, two):
        return jnp.where(one == two, 1.0, 0.0)

    def forward_flags():
        z1 = jnp.maximum(z - 1, 0)
        z2 = jnp.maximum(z - 2, 0)
        edge = last_of(z1, GROUP - 1)
        links = [flag(last_of(z, 0), edge)]
        for i in range(1, GROUP):
            links.append(flag(last_of(z, i), last_of(z, i - 1)))
        from_one = jnp.where(z >= 1, 1.0, 0.0)
        from_two = jnp.where(z >= 2, 1.0, 0.0) * flag(last_of(z2, GROUP - 1), edge)
        return links, from_one, from_two

    def backward_flags():
        z1 = jnp.minimum(z + 1, LINES - 1)
        z2 = jnp.minimum(z + 2, LINES - 1)
        edge = first_of(z1, 0)
        links = [None] * GROUP
        links[GROUP - 1] = flag(first_of(z, GROUP - 1), edge)
        for i in range(GROUP - 1):
            links[i] = flag(first_of(z, i), first_of(z, i + 1))
        from_one = jnp.where(z <= LINES - 2, 1.0, 0.0)
        from_two = jnp.where(z <= LINES - 3, 1.0, 0.0) * flag(first_of(z2, 0), edge)
        return links, from_one, from_two

    def line_total(j, landed, mine_r, far, steps, links, stage, slot, direction):
        run = landed[j, steps[0]].astype(F32)
        for i in steps[1:]:
            run = landed[j, i].astype(F32) + links[i] * run
        mine_r[j] = run.astype(BF16)
        for n in (0, 1):
            zt = lax.rem(z + LINES + direction * (n + 1), LINES)
            send(mine_r.at[j], far.at[j, n], stage, slot, ctx_of(zt, g), y)

    def line_carry(j, landed, far, steps, flags, out, back, stage, slot, recv_slot):
        links, from_one, from_two = flags
        took(far.at[j], recv_slot)
        run = from_one * far[j, 0].astype(F32) + from_two * far[j, 1].astype(F32)
        out[j, steps[0]] = run.astype(BF16)
        for n in range(GROUP - 1):
            i = steps[n]
            run = landed[j, i].astype(F32) + links[i] * run
            out[j, steps[n + 1]] = run.astype(BF16)
        for dg in G_ORDER:
            gt = g_peer(dg)
            send(out.at[j, gt], back.at[j, g], stage, slot, ctx_of(z, gt), y)
        back[j, g] = out[j, g]

    up = tuple(range(GROUP))
    down = tuple(reversed(range(GROUP)))

    def f_total(j):
        took(srf.at[j, 0 : GROUP - 1], state_slot + j)
        line_total(j, srf, rf, zrf, up, fwd[0], 4, state_slot + CHUNKS + j, 1)

    def f_carry(j):
        line_carry(j, srf, zrf, up, fwd, csf, crf, 5, state_slot + 2 * CHUNKS + j, state_slot + CHUNKS + j)

    def b_total(j):
        took(srb.at[j, 0 : GROUP - 1], state_slot + 3 * CHUNKS + j)
        line_total(j, srb, rb, zrb, down, bwd[0], 7, state_slot + 4 * CHUNKS + j, -1)

    def b_carry(j):
        line_carry(
            j, srb, zrb, down, bwd, csb, crb, 8, state_slot + 5 * CHUNKS + j, state_slot + 4 * CHUNKS + j
        )

    def carried(ref, j, hh):
        return ref[j, 2 * hh : 2 * hh + 2].reshape(HEAD_DIM, HEAD_DIM)

    def weigh(j):
        for hh in range(CHUNK_HEADS):
            qh, kh = q_of(j, hh), k_of(j, hh)
            weights = (nt(qh, kh) * vis[...]).astype(BF16)
            wt[CHUNK_HEADS * j + hh] = (nt(kh, qh) * vist[...]).astype(BF16)
            kg_part[j, :, lanes_of(hh)] = nn(weights, v_of(j, hh))

    def attend(j):
        took(crf.at[j, 0 : GROUP - 1], state_slot + 2 * CHUNKS + j)
        squares, inner = 0.0, 0.0
        for hh in range(CHUNK_HEADS):
            h = CHUNK_HEADS * j + hh
            cols = slice(HEAD_DIM * h, HEAD_DIM * (h + 1))
            carry = carried(crf, j, hh)
            out = kg_part[j, :, lanes_of(hh)] + resume[...] * nn(q_of(j, hh), carry)
            out = out.astype(BF16)
            att[j, :, lanes_of(hh)] = out
            out = out.astype(F32)
            scaled = ng[:, cols].astype(F32) * gain[:, cols].astype(F32)
            squares = squares + out * out
            inner = inner + scaled * out
        return squares, inner

    first_hop(0)
    took(seg_line.at[0 : LINES - 1], 0)
    seg_all[g] = seg_line[...]
    for dg in G_ORDER:
        send(seg_line, seg_all.at[g], 9, 1, ctx_of(z, g_peer(dg)), y)
    first_hop(1)
    second_hop(0)
    took(seg_all.at[0 : GROUP - 1], 1)
    fwd = forward_flags()
    bwd = backward_flags()
    before = jnp.maximum(me - 1, 0)
    after = jnp.minimum(me + 1, LINES * GROUP - 1)
    seg_rows = jnp.broadcast_to(seg[...].astype(F32), (ROWS, ROWS)).T
    resume[...] = jnp.where(seg_rows == last_of(lax.div(before, GROUP), lax.rem(before, GROUP)), 1.0, 0.0)
    reaches[...] = jnp.where(seg_rows == first_of(lax.div(after, GROUP), lax.rem(after, GROUP)), 1.0, 0.0)
    first_hop(2)
    second_hop(1)
    forward_state(0)
    first_hop(3)
    second_hop(2)
    f_total(0)
    first_hop(4)
    second_hop(3)
    forward_state(1)
    first_hop(5)
    f_carry(0)
    second_hop(4)
    first_hop(6)
    f_total(1)
    second_hop(5)
    forward_state(2)
    first_hop(7)
    f_carry(1)
    second_hop(6)
    weigh(0)
    first_hop(8)
    f_total(2)
    second_hop(7)
    weigh(1)
    ng_copy.wait()
    sums = [attend(0)]
    second_hop(8)
    weigh(2)
    f_carry(2)
    sums.append(attend(1))
    sums.append(attend(2))

    squares = sums[0][0] + sums[1][0] + sums[2][0]
    inner = sums[0][1] + sums[1][1] + sums[2][1]
    sq_send[0:1, :] = jnp.sum(squares.T, axis=0, keepdims=True)
    sq_send[1:2, :] = jnp.sum(inner.T, axis=0, keepdims=True)
    sq_slot = state_slot + 6 * CHUNKS
    for dy in range(1, HEAD_PEERS):
        send(sq_send, sq_recv.at[y], 10, sq_slot, me, lax.rem(y + dy, HEAD_PEERS))
    sq_recv[y] = sq_send[...]
    took(sq_recv.at[0 : HEAD_PEERS - 1], sq_slot)
    total = (sq_recv[0] + sq_recv[1]) + (sq_recv[2] + sq_recv[3])
    width = HEADS * HEAD_DIM
    inverse = lax.rsqrt(total[0:1, :] / width + 1e-05)
    projection = inverse * total[1:2, :] / width
    inverse = jnp.broadcast_to(inverse, (ROWS, ROWS)).T
    projection = jnp.broadcast_to(projection, (ROWS, ROWS)).T

    outs = []

    def put(ref, hbm, j, n):
        copy = pltpu.make_async_copy(ref.at[j], hbm.at[:, WIDE * j : WIDE * (j + 1)], out_sem.at[n, j])
        copy.start()
        outs.append(copy)

    for j in range(CHUNKS):
        for hh in range(CHUNK_HEADS):
            h = CHUNK_HEADS * j + hh
            cols = slice(HEAD_DIM * h, HEAD_DIM * (h + 1))
            gain_f = gain[:, cols].astype(F32)
            scaled = ng[:, cols].astype(F32) * gain_f
            normal = att[j, :, lanes_of(hh)].astype(F32) * inverse
            o_n[j, :, lanes_of(hh)] = (normal * gain_f).astype(BF16)
            gr[j, :, lanes_of(hh)] = (inverse * (scaled - normal * projection)).astype(BF16)
        backward_state(j)
    for j in range(CHUNKS):
        put(o_n, normed_hbm, j, 0)

    def partial(j):
        for hh in range(CHUNK_HEADS):
            h = CHUNK_HEADS * j + hh
            qh, kh, vh = q_of(j, hh), k_of(j, hh), v_of(j, hh)
            gh = gr[j, :, lanes_of(hh)]
            grads = (nt(gh, vh) * vis[...]).astype(BF16)
            grads_t = (nt(vh, gh) * vist[...]).astype(BF16)
            query = nn(grads, kh) + resume[...] * nt(gh, carried(crf, j, hh))
            o_q[j, :, lanes_of(hh)] = query.astype(BF16)
            kg_part[j, :, lanes_of(hh)] = nn(grads_t, qh)
            vg_part[j, :, lanes_of(hh)] = nn(wt[h], gh)
        put(o_q, qg_hbm, j, 1)

    def finish(j):
        took(crb.at[j, 0 : GROUP - 1], state_slot + 5 * CHUNKS + j)
        for hh in range(CHUNK_HEADS):
            back = carried(crb, j, hh)
            key = kg_part[j, :, lanes_of(hh)] + reaches[...] * nt(v_of(j, hh), back)
            o_k[j, :, lanes_of(hh)] = key.astype(BF16)
            value = vg_part[j, :, lanes_of(hh)] + reaches[...] * nn(k_of(j, hh), back)
            o_v[j, :, lanes_of(hh)] = value.astype(BF16)
        put(o_k, kg_hbm, j, 2)
        put(o_v, vg_hbm, j, 3)

    partial(0)
    b_total(0)
    partial(1)
    b_total(1)
    partial(2)
    b_total(2)
    for j in range(CHUNKS):
        b_carry(j)
    for j in range(CHUNKS):
        finish(j)

    def left(ref, stage):
        pltpu.make_async_copy(ref, ref, send_sem.at[stage]).wait()

    left(seg_line.at[0 : LINES - 1], 0)
    left(a.at[:, 0 : ROWS - BAND], 1)
    left(c.at[:, 0 : ROWS - BAND], 2)
    left(sf.at[:, 0 : GROUP - 1], 3)
    left(zrf, 4)
    left(csf.at[:, 0 : GROUP - 1], 5)
    left(sb.at[:, 0 : GROUP - 1], 6)
    left(zrb, 7)
    left(csb.at[:, 0 : GROUP - 1], 8)
    left(seg_all.at[0 : GROUP - 1], 9)
    left(sq_recv.at[0 : HEAD_PEERS - 1], 10)
    for copy in outs:
        copy.wait()


def shards(queries, keys, values, normed_grad, gain, segment, plan):
    vm = pltpu.VMEM
    parcels = vm((PARCELS, ROWS, WIDE), BF16)
    square = vm((ROWS, ROWS), F32)
    square_b = vm((ROWS, ROWS), BF16)
    chunked = vm((CHUNKS, ROWS, WIDE), BF16)
    chunked_f = vm((CHUNKS, ROWS, WIDE), F32)
    states = vm((CHUNKS, GROUP, SLICE, HEAD_DIM), BF16)
    state_set = [
        states, states, vm((CHUNKS, SLICE, HEAD_DIM), BF16), vm((CHUNKS, 2, SLICE, HEAD_DIM), BF16),
        states, states,
    ]
    weights = vm((OWN_HEADS, ROWS, ROWS), BF16)
    sums = vm((8, ROWS), F32)
    out = jax.ShapeDtypeStruct(queries.shape, BF16)
    return tuple(pl.pallas_call(
        kernel,
        out_shape=(out, out, out, out),
        in_specs=[pl.BlockSpec(memory_space=pl.ANY)] * 7,
        out_specs=[pl.BlockSpec(memory_space=pl.ANY)] * 4,
        scratch_shapes=[
            parcels, parcels, parcels, parcels, parcels, parcels,
            vm((ROWS, OWN_HEADS * HEAD_DIM), BF16), vm((1, OWN_HEADS * HEAD_DIM), BF16),
            vm((1, ROWS), jnp.int32), vm((LINES * GROUP, ROWS), jnp.int32),
            vm((LINES, 2, ROWS), F32), vm((GROUP, LINES, 2, ROWS), F32),
            square_b, square_b, square, square, square_b, square_b, square, square,
            *state_set, *state_set,
            chunked, chunked, weights, weights, sums, vm((HEAD_PEERS, 8, ROWS), F32),
            chunked_f, chunked_f, chunked, chunked, chunked, chunked,
            pltpu.SemaphoreType.DMA((PARCELS + 4,)),
            pltpu.SemaphoreType.DMA((4, CHUNKS)),
            pltpu.SemaphoreType.DMA((2,)),
            pltpu.SemaphoreType.DMA((11,)),
            pltpu.SemaphoreType.DMA((2 + 2 * PARCELS + 6 * CHUNKS + 1,)),
        ],
        compiler_params=pltpu.CompilerParams(
            collective_id=0, has_side_effects=True, vmem_limit_bytes=48 << 20
        ),
    )(
        queries, keys, values, normed_grad,
        gain.reshape(1, -1), segment.reshape(1, -1), plan.reshape(LINES * GROUP, ROWS),
    ))


def solution(mesh):
    both = P("ctx", "head")
    return jax.shard_map(
        shards,
        mesh=mesh,
        in_specs=(both, both, both, both, P("head"), P("ctx"), P()),
        out_specs=(both, both, both, both),
        check_vma=False,
    )
```

```python
import jax
import jax.numpy as jnp
from jax import lax
from jax.experimental import pallas as pl
from jax.experimental.pallas import tpu as pltpu
from jax.sharding import PartitionSpec as P

HEADS = 48
HEAD_DIM = 128
ROWS = 128
LINES = 8
GROUP = 8
OWN_HEADS = 12
CHUNKS = 3
CHUNK_HEADS = OWN_HEADS // CHUNKS
WIDE = CHUNK_HEADS * HEAD_DIM
PARCELS = 3 * CHUNKS
BAND = ROWS // LINES
SLICE = WIDE // GROUP
HEAD_PEERS = 4
MESH = pl.DeviceIdType.MESH
F32 = jnp.float32
BF16 = jnp.bfloat16
Z_ORDER = (4, 3, 5, 2, 6, 1, 7)
G_ORDER = (4, 3, 5, 2, 6, 1, 7)


def nn(a, b):
    return lax.dot_general(a, b, (((1,), (0,)), ((), ())), preferred_element_type=F32)


def nt(a, b):
    return lax.dot_general(a, b, (((1,), (1,)), ((), ())), preferred_element_type=F32)


def tn(a, b):
    return lax.dot_general(a, b, (((0,), (0,)), ((), ())), preferred_element_type=F32)


def iota(dim):
    return lax.broadcasted_iota(jnp.int32, (ROWS, ROWS), dim)


def kernel(
    q_hbm, k_hbm, v_hbm, ng_hbm, gain_hbm, seg_hbm, plan_hbm,
    o_n, o_q, o_k, o_v,
    x, a, b, c, d, seq, ng, gain, seg, plan,
    seg_line, seg_all, mid, settle, vis, vist, tails, heads, resume, reaches,
    sf, srf, rf, zrf, csf, crf, sb, srb, rb, zrb, csb, crb,
    att, gr, wt, sq_send, sq_recv, kg_part, vg_part,
    load_sem, send_sem, recv_sem,
):
    me = lax.axis_index("ctx")
    y = lax.axis_index("head")
    z = lax.div(me, GROUP)
    g = lax.rem(me, GROUP)

    def z_peer(dz):
        return lax.rem(z + dz, LINES)

    def g_peer(dg):
        return lax.rem(g + dg, GROUP)

    def ctx_of(zz, gg):
        return zz * GROUP + gg

    def band(i):
        return pl.ds(pl.multiple_of(i * BAND, BAND), BAND)

    def send(src, dst, stage, slot, ctx_to, head_to):
        pltpu.make_async_remote_copy(
            src_ref=src, dst_ref=dst, send_sem=send_sem.at[stage], recv_sem=recv_sem.at[slot],
            device_id=(ctx_to, head_to), device_id_type=MESH,
        ).start()

    def took(ref, slot):
        pltpu.make_async_copy(ref, ref, recv_sem.at[slot]).wait()

    barrier = pltpu.get_barrier_semaphore()
    for dz in Z_ORDER:
        pl.semaphore_signal(barrier, inc=1, device_id=(ctx_of(z_peer(dz), g), y), device_id_type=MESH)
    for dg in G_ORDER:
        pl.semaphore_signal(barrier, inc=1, device_id=(ctx_of(z, g_peer(dg)), y), device_id_type=MESH)
    for dy in range(1, HEAD_PEERS):
        pl.semaphore_signal(
            barrier, inc=1, device_id=(me, lax.rem(y + dy, HEAD_PEERS)), device_id_type=MESH
        )

    order = []
    for j in range(CHUNKS):
        order.append((k_hbm, j))
        order.append((v_hbm, j))
    for j in range(CHUNKS):
        order.append((q_hbm, j))
    plan_copy = pltpu.make_async_copy(plan_hbm, plan, load_sem.at[PARCELS])
    plan_copy.start()
    seg_copy = pltpu.make_async_copy(seg_hbm, seg, load_sem.at[PARCELS + 1])
    seg_copy.start()
    loads = []
    for p, (ref, j) in enumerate(order):
        copy = pltpu.make_async_copy(ref.at[:, WIDE * j : WIDE * (j + 1)], x.at[p], load_sem.at[p])
        copy.start()
        loads.append(copy)
    gain_copy = pltpu.make_async_copy(gain_hbm, gain, load_sem.at[PARCELS + 2])
    gain_copy.start()
    ng_copy = pltpu.make_async_copy(ng_hbm, ng, load_sem.at[PARCELS + 3])
    ng_copy.start()

    plan_copy.wait()
    rows_i = iota(0)
    cols_i = iota(1)
    own_plan = plan[pl.ds(me, 1), :]
    slot_of = 2 * lax.shift_right_logical(own_plan, 7) + (cols_i[0:1, :] & 1)
    leave = (rows_i == slot_of).astype(F32).astype(BF16)

    def sort(p):
        loads[p].wait()
        a[p] = nn(leave, x[p]).astype(BF16)

    def depart(p):
        for dz in Z_ORDER:
            zt = z_peer(dz)
            send(a.at[p, band(zt)], b.at[p, band(z)], 1, 2 + p, ctx_of(zt, g), y)
        b[p, band(z), :] = a[p, band(z), :]

    seg_copy.wait()
    seg_f = seg[...].astype(F32)
    last_here = jnp.broadcast_to(seg_f[:, ROWS - 1 : ROWS], (1, ROWS))
    first_here = jnp.broadcast_to(seg_f[:, 0:1], (1, ROWS))
    seg_line[z, 0:1, :] = last_here
    seg_line[z, 1:2, :] = first_here
    sort(0)

    pl.semaphore_wait(barrier, LINES - 1 + GROUP - 1 + HEAD_PEERS - 1)

    depart(0)
    for dz in Z_ORDER:
        send(seg_line.at[z], seg_line.at[z], 0, 0, ctx_of(z_peer(dz), g), y)
    for p in range(1, 2 * CHUNKS + 1):
        sort(p)
        depart(p)
    for p in range(2 * CHUNKS + 1, PARCELS):
        sort(p)

    seg_lanes = jnp.broadcast_to(seg_f, (ROWS, ROWS))
    seg_rows = seg_lanes.T
    same = seg_lanes == seg_rows
    vis[...] = jnp.where(same & (rows_i >= cols_i), 1.0, 0.0)
    vist[...] = jnp.where(same & (cols_i >= rows_i), 1.0, 0.0)
    tails[...] = jnp.where(seg_rows == last_here, 1.0, 0.0).astype(BF16)
    heads[...] = jnp.where(seg_rows == first_here, 1.0, 0.0).astype(BF16)

    source = ((rows_i & 15) >> 1) * BAND + (rows_i >> 4) * 2 + (rows_i & 1)
    mid[...] = (cols_i == source).astype(F32).astype(BF16)
    plan_all = plan[...]
    lanes = lax.broadcasted_iota(jnp.int32, (LINES * GROUP, ROWS), 1)
    mine = (lax.shift_right_logical(plan_all, 7) == me) & ((lanes & 1) == 0)
    start = jnp.sum(jnp.where(mine, (plan_all & 127).astype(F32), 0.0), axis=1, keepdims=True)
    start = jnp.broadcast_to(start, (LINES * GROUP, ROWS)).astype(BF16)
    pick_rows = lax.broadcasted_iota(jnp.int32, (ROWS, LINES * GROUP), 0)
    pick_cols = lax.broadcasted_iota(jnp.int32, (ROWS, LINES * GROUP), 1)
    pick = (pick_cols == ((pick_rows & 15) >> 1) * GROUP + (pick_rows >> 4)).astype(F32).astype(BF16)
    place = nn(pick, start) + (rows_i & 1).astype(F32)
    settle[...] = jnp.where(cols_i.astype(F32) == place, 1.0, 0.0).T.astype(BF16)

    def first_hop(p):
        took(b.at[p, 0 : ROWS - BAND], 2 + p)
        c[p] = nn(mid[...], b[p]).astype(BF16)
        for dg in G_ORDER:
            gt = g_peer(dg)
            send(c.at[p, band(gt)], d.at[p, band(g)], 2, 2 + PARCELS + p, ctx_of(z, gt), y)
        d[p, band(g), :] = c[p, band(g), :]

    def second_hop(p):
        took(d.at[p, 0 : ROWS - BAND], 2 + PARCELS + p)
        seq[p] = nn(settle[...], d[p]).astype(BF16)

    def lanes_of(hh):
        return slice(HEAD_DIM * hh, HEAD_DIM * (hh + 1))

    def k_of(j, hh):
        return seq[2 * j, :, lanes_of(hh)]

    def v_of(j, hh):
        return seq[2 * j + 1, :, lanes_of(hh)]

    def q_of(j, hh):
        return seq[2 * CHUNKS + j, :, lanes_of(hh)]

    state_slot = 2 + 2 * PARCELS

    def spread(j, local, landed, stage, slot):
        for dg in G_ORDER:
            gt = g_peer(dg)
            send(local.at[j, gt], landed.at[j, g], stage, slot, ctx_of(z, gt), y)
        landed[j, g] = local[j, g]

    def forward_state(j):
        for hh in range(CHUNK_HEADS):
            state = tn(k_of(j, hh) * tails[...], v_of(j, hh)).astype(BF16)
            sf[j, 2 * hh : 2 * hh + 2] = state.reshape(2, SLICE, HEAD_DIM)
        spread(j, sf, srf, 3, state_slot + j)

    def backward_state(j):
        for hh in range(CHUNK_HEADS):
            state = tn(q_of(j, hh) * heads[...], gr[j, :, lanes_of(hh)]).astype(BF16)
            sb[j, 2 * hh : 2 * hh + 2] = state.reshape(2, SLICE, HEAD_DIM)
        spread(j, sb, srb, 6, state_slot + 3 * CHUNKS + j)

    def last_of(zz, gg):
        return seg_all[gg, zz, 0:1, :]

    def first_of(zz, gg):
        return seg_all[gg, zz, 1:2, :]

    def flag(one, two):
        return jnp.where(one == two, 1.0, 0.0)

    def forward_flags():
        z1 = jnp.maximum(z - 1, 0)
        z2 = jnp.maximum(z - 2, 0)
        edge = last_of(z1, GROUP - 1)
        links = [flag(last_of(z, 0), edge)]
        for i in range(1, GROUP):
            links.append(flag(last_of(z, i), last_of(z, i - 1)))
        from_one = jnp.where(z >= 1, 1.0, 0.0)
        from_two = jnp.where(z >= 2, 1.0, 0.0) * flag(last_of(z2, GROUP - 1), edge)
        return links, from_one, from_two

    def backward_flags():
        z1 = jnp.minimum(z + 1, LINES - 1)
        z2 = jnp.minimum(z + 2, LINES - 1)
        edge = first_of(z1, 0)
        links = [None] * GROUP
        links[GROUP - 1] = flag(first_of(z, GROUP - 1), edge)
        for i in range(GROUP - 1):
            links[i] = flag(first_of(z, i), first_of(z, i + 1))
        from_one = jnp.where(z <= LINES - 2, 1.0, 0.0)
        from_two = jnp.where(z <= LINES - 3, 1.0, 0.0) * flag(first_of(z2, 0), edge)
        return links, from_one, from_two

    def line_total(j, landed, mine_r, far, steps, links, stage, slot, direction):
        run = landed[j, steps[0]].astype(F32)
        for i in steps[1:]:
            run = landed[j, i].astype(F32) + links[i] * run
        mine_r[j] = run.astype(BF16)
        for n in (0, 1):
            zt = lax.rem(z + LINES + direction * (n + 1), LINES)
            send(mine_r.at[j], far.at[j, n], stage, slot, ctx_of(zt, g), y)

    def line_carry(j, landed, far, steps, flags, out, back, stage, slot, recv_slot):
        links, from_one, from_two = flags
        took(far.at[j], recv_slot)
        run = from_one * far[j, 0].astype(F32) + from_two * far[j, 1].astype(F32)
        out[j, steps[0]] = run.astype(BF16)
        for n in range(GROUP - 1):
            i = steps[n]
            run = landed[j, i].astype(F32) + links[i] * run
            out[j, steps[n + 1]] = run.astype(BF16)
        for dg in G_ORDER:
            gt = g_peer(dg)
            send(out.at[j, gt], back.at[j, g], stage, slot, ctx_of(z, gt), y)
        back[j, g] = out[j, g]

    up = tuple(range(GROUP))
    down = tuple(reversed(range(GROUP)))

    def f_total(j):
        took(srf.at[j, 0 : GROUP - 1], state_slot + j)
        line_total(j, srf, rf, zrf, up, fwd[0], 4, state_slot + CHUNKS + j, 1)

    def f_carry(j):
        line_carry(j, srf, zrf, up, fwd, csf, crf, 5, state_slot + 2 * CHUNKS + j, state_slot + CHUNKS + j)

    def b_total(j):
        took(srb.at[j, 0 : GROUP - 1], state_slot + 3 * CHUNKS + j)
        line_total(j, srb, rb, zrb, down, bwd[0], 7, state_slot + 4 * CHUNKS + j, -1)

    def b_carry(j):
        line_carry(
            j, srb, zrb, down, bwd, csb, crb, 8, state_slot + 5 * CHUNKS + j, state_slot + 4 * CHUNKS + j
        )

    def carried(ref, j, hh):
        return ref[j, 2 * hh : 2 * hh + 2].reshape(HEAD_DIM, HEAD_DIM)

    def weigh(j):
        for hh in range(CHUNK_HEADS):
            qh, kh = q_of(j, hh), k_of(j, hh)
            weights = (nt(qh, kh) * vis[...]).astype(BF16)
            wt[CHUNK_HEADS * j + hh] = (nt(kh, qh) * vist[...]).astype(BF16)
            kg_part[j, :, lanes_of(hh)] = nn(weights, v_of(j, hh))

    def attend(j):
        took(crf.at[j, 0 : GROUP - 1], state_slot + 2 * CHUNKS + j)
        squares, inner = 0.0, 0.0
        for hh in range(CHUNK_HEADS):
            h = CHUNK_HEADS * j + hh
            cols = slice(HEAD_DIM * h, HEAD_DIM * (h + 1))
            carry = carried(crf, j, hh)
            out = kg_part[j, :, lanes_of(hh)] + resume[...] * nn(q_of(j, hh), carry)
            out = out.astype(BF16)
            att[j, :, lanes_of(hh)] = out
            out = out.astype(F32)
            scaled = ng[:, cols].astype(F32) * gain[:, cols].astype(F32)
            squares = squares + out * out
            inner = inner + scaled * out
        return squares, inner

    first_hop(0)
    took(seg_line.at[0 : LINES - 1], 0)
    seg_all[g] = seg_line[...]
    for dg in G_ORDER:
        send(seg_line, seg_all.at[g], 9, 1, ctx_of(z, g_peer(dg)), y)
    first_hop(1)
    second_hop(0)
    took(seg_all.at[0 : GROUP - 1], 1)
    fwd = forward_flags()
    bwd = backward_flags()
    before = jnp.maximum(me - 1, 0)
    after = jnp.minimum(me + 1, LINES * GROUP - 1)
    seg_rows = jnp.broadcast_to(seg[...].astype(F32), (ROWS, ROWS)).T
    resume[...] = jnp.where(seg_rows == last_of(lax.div(before, GROUP), lax.rem(before, GROUP)), 1.0, 0.0)
    reaches[...] = jnp.where(seg_rows == first_of(lax.div(after, GROUP), lax.rem(after, GROUP)), 1.0, 0.0)
    first_hop(2)
    second_hop(1)
    forward_state(0)
    first_hop(3)
    second_hop(2)
    first_hop(4)
    f_total(0)
    depart(7)
    second_hop(3)
    forward_state(1)
    first_hop(5)
    second_hop(4)
    f_total(1)
    depart(8)
    f_carry(0)
    first_hop(6)
    second_hop(5)
    forward_state(2)
    f_carry(1)
    second_hop(6)
    weigh(0)
    first_hop(7)
    f_total(2)
    gain_copy.wait()
    ng_copy.wait()
    sums = [attend(0)]
    second_hop(7)
    weigh(1)
    first_hop(8)
    f_carry(2)
    sums.append(attend(1))
    second_hop(8)
    weigh(2)
    sums.append(attend(2))

    squares = sums[0][0] + sums[1][0] + sums[2][0]
    inner = sums[0][1] + sums[1][1] + sums[2][1]
    sq_send[0:1, :] = jnp.sum(squares.T, axis=0, keepdims=True)
    sq_send[1:2, :] = jnp.sum(inner.T, axis=0, keepdims=True)
    sq_slot = state_slot + 6 * CHUNKS
    for dy in range(1, HEAD_PEERS):
        send(sq_send, sq_recv.at[y], 10, sq_slot, me, lax.rem(y + dy, HEAD_PEERS))
    sq_recv[y] = sq_send[...]
    took(sq_recv.at[0 : HEAD_PEERS - 1], sq_slot)
    total = (sq_recv[0] + sq_recv[1]) + (sq_recv[2] + sq_recv[3])
    width = HEADS * HEAD_DIM
    inverse = lax.rsqrt(total[0:1, :] / width + 1e-05)
    projection = inverse * total[1:2, :] / width
    inverse = jnp.broadcast_to(inverse, (ROWS, ROWS)).T
    projection = jnp.broadcast_to(projection, (ROWS, ROWS)).T

    for j in range(CHUNKS):
        for hh in range(CHUNK_HEADS):
            h = CHUNK_HEADS * j + hh
            cols = slice(HEAD_DIM * h, HEAD_DIM * (h + 1))
            scaled = ng[:, cols].astype(F32) * gain[:, cols].astype(F32)
            normal = att[j, :, lanes_of(hh)].astype(F32) * inverse
            gr[j, :, lanes_of(hh)] = (inverse * (scaled - normal * projection)).astype(BF16)
        backward_state(j)

    def norm(j):
        for hh in range(CHUNK_HEADS):
            h = CHUNK_HEADS * j + hh
            normal = att[j, :, lanes_of(hh)].astype(F32) * inverse
            gain_f = gain[:, HEAD_DIM * h : HEAD_DIM * (h + 1)].astype(F32)
            o_n[j, :, lanes_of(hh)] = (normal * gain_f).astype(BF16)

    def partial(j):
        for hh in range(CHUNK_HEADS):
            h = CHUNK_HEADS * j + hh
            qh, kh, vh = q_of(j, hh), k_of(j, hh), v_of(j, hh)
            gh = gr[j, :, lanes_of(hh)]
            grads = (nt(gh, vh) * vis[...]).astype(BF16)
            grads_t = (nt(vh, gh) * vist[...]).astype(BF16)
            query = nn(grads, kh) + resume[...] * nt(gh, carried(crf, j, hh))
            o_q[j, :, lanes_of(hh)] = query.astype(BF16)
            kg_part[j, :, lanes_of(hh)] = nn(grads_t, qh)
            vg_part[j, :, lanes_of(hh)] = nn(wt[h], gh)

    def finish(j):
        took(crb.at[j, 0 : GROUP - 1], state_slot + 5 * CHUNKS + j)
        for hh in range(CHUNK_HEADS):
            back = carried(crb, j, hh)
            key = kg_part[j, :, lanes_of(hh)] + reaches[...] * nt(v_of(j, hh), back)
            o_k[j, :, lanes_of(hh)] = key.astype(BF16)
            value = vg_part[j, :, lanes_of(hh)] + reaches[...] * nn(k_of(j, hh), back)
            o_v[j, :, lanes_of(hh)] = value.astype(BF16)

    norm(0)
    norm(1)
    norm(2)
    partial(0)
    partial(1)
    b_total(0)
    b_total(1)
    b_total(2)
    partial(2)
    for j in range(CHUNKS):
        b_carry(j)
    for j in range(CHUNKS):
        finish(j)

    def left(ref, stage):
        pltpu.make_async_copy(ref, ref, send_sem.at[stage]).wait()

    left(seg_line.at[0 : LINES - 1], 0)
    left(a.at[:, 0 : ROWS - BAND], 1)
    left(c.at[:, 0 : ROWS - BAND], 2)
    left(sf.at[:, 0 : GROUP - 1], 3)
    left(zrf, 4)
    left(csf.at[:, 0 : GROUP - 1], 5)
    left(sb.at[:, 0 : GROUP - 1], 6)
    left(zrb, 7)
    left(csb.at[:, 0 : GROUP - 1], 8)
    left(seg_all.at[0 : GROUP - 1], 9)
    left(sq_recv.at[0 : HEAD_PEERS - 1], 10)


def deliver(n_in, q_in, k_in, v_in, n_out, q_out, k_out, v_out, sem):
    copies = []
    for i, (src, dst) in enumerate(((n_in, n_out), (q_in, q_out), (k_in, k_out), (v_in, v_out))):
        for j in range(CHUNKS):
            copy = pltpu.make_async_copy(src.at[j], dst.at[:, WIDE * j : WIDE * (j + 1)], sem.at[i, j])
            copy.start()
            copies.append(copy)
    for copy in copies:
        copy.wait()


def shards(queries, keys, values, normed_grad, gain, segment, plan):
    vm = pltpu.VMEM
    parcels = vm((PARCELS, ROWS, WIDE), BF16)
    square = vm((ROWS, ROWS), F32)
    square_b = vm((ROWS, ROWS), BF16)
    chunked = vm((CHUNKS, ROWS, WIDE), BF16)
    chunked_f = vm((CHUNKS, ROWS, WIDE), F32)
    states = vm((CHUNKS, GROUP, SLICE, HEAD_DIM), BF16)
    state_set = [
        states, states, vm((CHUNKS, SLICE, HEAD_DIM), BF16), vm((CHUNKS, 2, SLICE, HEAD_DIM), BF16),
        states, states,
    ]
    weights = vm((OWN_HEADS, ROWS, ROWS), BF16)
    sums = vm((8, ROWS), F32)
    out = vm((CHUNKS, ROWS, WIDE), BF16)
    inputs = (
        queries, keys, values, normed_grad,
        gain.reshape(1, -1), segment.reshape(1, -1), plan.reshape(LINES * GROUP, ROWS),
    )
    results = pl.pallas_call(
        kernel,
        out_shape=(out, out, out, out),
        in_specs=[pl.BlockSpec(memory_space=pltpu.HBM)] * 7,
        out_specs=[pl.BlockSpec(memory_space=pltpu.VMEM)] * 4,
        scratch_shapes=[
            parcels, parcels, parcels, parcels, parcels, parcels,
            vm((ROWS, OWN_HEADS * HEAD_DIM), BF16), vm((1, OWN_HEADS * HEAD_DIM), BF16),
            vm((1, ROWS), jnp.int32), vm((LINES * GROUP, ROWS), jnp.int32),
            vm((LINES, 2, ROWS), F32), vm((GROUP, LINES, 2, ROWS), F32),
            square_b, square_b, square, square, square_b, square_b, square, square,
            *state_set, *state_set,
            chunked, chunked, weights, sums, vm((HEAD_PEERS, 8, ROWS), F32),
            chunked_f, chunked_f,
            pltpu.SemaphoreType.DMA((PARCELS + 4,)),
            pltpu.SemaphoreType.DMA((11,)),
            pltpu.SemaphoreType.DMA((2 + 2 * PARCELS + 6 * CHUNKS + 1,)),
        ],
        compiler_params=pltpu.CompilerParams(
            collective_id=0, has_side_effects=True, vmem_limit_bytes=40 << 20
        ),
    )(*(pltpu.with_memory_space_constraint(t, pltpu.HBM) for t in inputs))
    final = jax.ShapeDtypeStruct(queries.shape, BF16)
    return tuple(pl.pallas_call(
        deliver,
        out_shape=(final, final, final, final),
        in_specs=[pl.BlockSpec(memory_space=pltpu.VMEM)] * 4,
        out_specs=[pl.BlockSpec(memory_space=pltpu.HBM)] * 4,
        scratch_shapes=[pltpu.SemaphoreType.DMA((4, CHUNKS))],
    )(*(pltpu.with_memory_space_constraint(t, pltpu.VMEM) for t in results)))


def solution(mesh):
    both = P("ctx", "head")
    return jax.shard_map(
        shards,
        mesh=mesh,
        in_specs=(both, both, both, both, P("head"), P("ctx"), P()),
        out_specs=(both, both, both, both),
        check_vma=False,
    )
```

```python
import jax
import jax.numpy as jnp
from jax import lax
from jax.experimental import pallas as pl
from jax.experimental.pallas import tpu as pltpu
from jax.sharding import PartitionSpec as P

HEADS = 48
HEAD_DIM = 128
ROWS = 128
LINES = 8
GROUP = 8
OWN_HEADS = 12
AHEAD = (4, 4, 3, 1)
BACK = (2, 4, 4, 2)
BAND = ROWS // LINES
PIECE = HEAD_DIM // GROUP
HEAD_PEERS = 4
MESH = pl.DeviceIdType.MESH
F32 = jnp.float32
BF16 = jnp.bfloat16
Z_ORDER = (4, 3, 5, 2, 6, 1, 7)
G_ORDER = (4, 3, 5, 2, 6, 1, 7)

KEY, VALUE, QUERY = 0, 1, 2
PARCELS = [(t, j) for j in range(len(AHEAD)) for t in (KEY, VALUE)]
PARCELS += [(QUERY, j) for j in range(len(AHEAD))]


def spans(chunks):
    firsts = [sum(chunks[:j]) for j in range(len(chunks))]
    return [range(f, f + n) for f, n in zip(firsts, chunks)]


AHEAD_SPANS = spans(AHEAD)
BACK_SPANS = spans(BACK)
PLACE = {h: (j, h - span[0]) for j, span in enumerate(AHEAD_SPANS) for h in span}


def timeline():
    wire_z, late_z, wire_x, late_x, wire_line, late_line = 0.7, 4.0, 0.36, 3.5, 0.2, 3.3
    events, second, clock = [], {}, 0.0
    for p, (t, j) in enumerate(PARCELS):
        clock += wire_z * AHEAD[j]
        first = clock + late_z
        events.append((first, "first_hop", p))
        second[t, j] = first + late_x + wire_x * AHEAD[j]
        events.append((second[t, j], "second_hop", p))
    for j, heads in enumerate(AHEAD):
        ready = second[VALUE, j] + 0.01
        events.append((ready, "forward_state", j))
        ready += late_x + (wire_x + 0.1) * heads
        events.append((ready, "f_total", j))
        clock = max(clock, ready) + wire_line * heads
        ready = clock + late_line
        events.append((ready, "f_carry", j))
        ready = max(ready + late_x + wire_x * heads, second[QUERY, j] + 0.02)
        events.append((second[QUERY, j] + 0.01, "weigh", j))
        events.append((ready, "attend", j))
    return [event[1:] for event in sorted(events)]


def nn(a, b):
    return lax.dot_general(a, b, (((1,), (0,)), ((), ())), preferred_element_type=F32)


def nt(a, b):
    return lax.dot_general(a, b, (((1,), (1,)), ((), ())), preferred_element_type=F32)


def tn(a, b):
    return lax.dot_general(a, b, (((0,), (0,)), ((), ())), preferred_element_type=F32)


def iota(dim):
    return lax.broadcasted_iota(jnp.int32, (ROWS, ROWS), dim)


def kernel(
    q_hbm, k_hbm, v_hbm, ng_hbm, gain_hbm, seg_hbm, plan_hbm,
    o_n, o_q, o_k, o_v,
    x, a, b, c, d, seq, ng, gain, gain_rows, seg, plan,
    seg_line, seg_all, mid, settle, vis, vist, tails, heads, resume, reaches,
    sf, srf, rf, zrf, csf, crf, sb, srb, rb, zrb, csb, crb,
    att, gr, wt, sq_send, sq_recv, kg_part, vg_part,
    load_sem, send_sem, hop_sem, state_sem, small_sem,
):
    me = lax.axis_index("ctx")
    y = lax.axis_index("head")
    z = lax.div(me, GROUP)
    g = lax.rem(me, GROUP)

    def z_peer(dz):
        return lax.rem(z + dz, LINES)

    def g_peer(dg):
        return lax.rem(g + dg, GROUP)

    def ctx_of(zz, gg):
        return zz * GROUP + gg

    def band(i):
        return pl.ds(pl.multiple_of(i * BAND, BAND), BAND)

    def send(src, dst, stage, sem, ctx_to, head_to):
        pltpu.make_async_remote_copy(
            src_ref=src, dst_ref=dst, send_sem=send_sem.at[stage], recv_sem=sem,
            device_id=(ctx_to, head_to), device_id_type=MESH,
        ).start()

    def took(ref, sem):
        pltpu.make_async_copy(ref, ref, sem).wait()

    barrier = pltpu.get_barrier_semaphore()
    for dz in Z_ORDER:
        pl.semaphore_signal(barrier, inc=1, device_id=(ctx_of(z_peer(dz), g), y), device_id_type=MESH)
    for dg in G_ORDER:
        pl.semaphore_signal(barrier, inc=1, device_id=(ctx_of(z, g_peer(dg)), y), device_id_type=MESH)
    for dy in range(1, HEAD_PEERS):
        pl.semaphore_signal(
            barrier, inc=1, device_id=(me, lax.rem(y + dy, HEAD_PEERS)), device_id_type=MESH
        )

    plan_copy = pltpu.make_async_copy(plan_hbm, plan, load_sem.at[len(PARCELS)])
    plan_copy.start()
    seg_copy = pltpu.make_async_copy(seg_hbm, seg, load_sem.at[len(PARCELS) + 1])
    seg_copy.start()
    loads = []
    for p, (t, j) in enumerate(PARCELS):
        span = AHEAD_SPANS[j]
        cols = slice(span.start * HEAD_DIM, span.stop * HEAD_DIM)
        copy = pltpu.make_async_copy((k_hbm, v_hbm, q_hbm)[t].at[:, cols], x[j].at[t], load_sem.at[p])
        copy.start()
        loads.append(copy)
    gain_copy = pltpu.make_async_copy(gain_hbm, gain, load_sem.at[len(PARCELS) + 2])
    gain_copy.start()
    ng_copy = pltpu.make_async_copy(ng_hbm, ng, load_sem.at[len(PARCELS) + 3])
    ng_copy.start()

    plan_copy.wait()
    rows_i = iota(0)
    cols_i = iota(1)
    own_plan = plan[pl.ds(me, 1), :]
    slot_of = 2 * lax.shift_right_logical(own_plan, 7) + (cols_i[0:1, :] & 1)
    leave = (rows_i == slot_of).astype(F32).astype(BF16)

    def sort(p):
        t, j = PARCELS[p]
        loads[p].wait()
        a[j][t] = nn(leave, x[j][t]).astype(BF16)

    def depart(p):
        t, j = PARCELS[p]
        for dz in Z_ORDER:
            zt = z_peer(dz)
            send(a[j].at[t, band(zt)], b[j].at[t, band(z)], 0, hop_sem.at[0, p], ctx_of(zt, g), y)
        b[j][t, band(z), :] = a[j][t, band(z), :]

    seg_copy.wait()
    seg_f = seg[...].astype(F32)
    last_here = jnp.broadcast_to(seg_f[:, ROWS - 1 : ROWS], (1, ROWS))
    first_here = jnp.broadcast_to(seg_f[:, 0:1], (1, ROWS))
    seg_line[z, 0:1, :] = last_here
    seg_line[z, 1:2, :] = first_here
    sort(0)

    pl.semaphore_wait(barrier, LINES - 1 + GROUP - 1 + HEAD_PEERS - 1)

    for dz in Z_ORDER:
        send(seg_line.at[z], seg_line.at[z], 1, small_sem.at[0], ctx_of(z_peer(dz), g), y)
    depart(0)
    for p, (t, j) in enumerate(PARCELS):
        if p > 0:
            sort(p)
            depart(p)

    seg_lanes = jnp.broadcast_to(seg_f, (ROWS, ROWS))
    seg_rows = seg_lanes.T
    same = seg_lanes == seg_rows
    vis[...] = jnp.where(same & (rows_i >= cols_i), 1.0, 0.0)
    vist[...] = jnp.where(same & (cols_i >= rows_i), 1.0, 0.0)
    tails[...] = jnp.where(seg_rows == last_here, 1.0, 0.0).astype(BF16)
    heads[...] = jnp.where(seg_rows == first_here, 1.0, 0.0).astype(BF16)

    source = ((rows_i & 15) >> 1) * BAND + (rows_i >> 4) * 2 + (rows_i & 1)
    mid[...] = (cols_i == source).astype(F32).astype(BF16)
    plan_all = plan[...]
    lanes = lax.broadcasted_iota(jnp.int32, (LINES * GROUP, ROWS), 1)
    mine = (lax.shift_right_logical(plan_all, 7) == me) & ((lanes & 1) == 0)
    start = jnp.sum(jnp.where(mine, (plan_all & 127).astype(F32), 0.0), axis=1, keepdims=True)
    start = jnp.broadcast_to(start, (LINES * GROUP, ROWS)).astype(BF16)
    pick_rows = lax.broadcasted_iota(jnp.int32, (ROWS, LINES * GROUP), 0)
    pick_cols = lax.broadcasted_iota(jnp.int32, (ROWS, LINES * GROUP), 1)
    pick = (pick_cols == ((pick_rows & 15) >> 1) * GROUP + (pick_rows >> 4)).astype(F32).astype(BF16)
    place = nn(pick, start) + (rows_i & 1).astype(F32)
    settle[...] = jnp.where(cols_i.astype(F32) == place, 1.0, 0.0).T.astype(BF16)

    def first_hop(p):
        t, j = PARCELS[p]
        took(b[j].at[t, 0 : ROWS - BAND], hop_sem.at[0, p])
        c[j][t] = nn(mid[...], b[j][t]).astype(BF16)
        for dg in G_ORDER:
            gt = g_peer(dg)
            send(c[j].at[t, band(gt)], d[j].at[t, band(g)], 2, hop_sem.at[1, p], ctx_of(z, gt), y)
        d[j][t, band(g), :] = c[j][t, band(g), :]
        if p == 0:
            took(seg_line.at[0 : LINES - 1], small_sem.at[0])
            seg_all[g] = seg_line[...]
            for dg in G_ORDER:
                send(seg_line, seg_all.at[g], 3, small_sem.at[1], ctx_of(z, g_peer(dg)), y)

    def second_hop(p):
        t, j = PARCELS[p]
        took(d[j].at[t, 0 : ROWS - BAND], hop_sem.at[1, p])
        seq[j][t] = nn(settle[...], d[j][t]).astype(BF16)

    def rows_of(t, h):
        j, hh = PLACE[h]
        return seq[j][t, :, HEAD_DIM * hh : HEAD_DIM * (hh + 1)]

    def columns(h):
        return slice(HEAD_DIM * h, HEAD_DIM * (h + 1))

    def spread(local, landed, stage, sem):
        for dg in G_ORDER:
            gt = g_peer(dg)
            send(local.at[gt], landed.at[g], stage, sem, ctx_of(z, gt), y)
        landed[g] = local[g]

    def forward_state(j):
        for hh, h in enumerate(AHEAD_SPANS[j]):
            state = tn(rows_of(KEY, h) * tails[...], rows_of(VALUE, h)).astype(BF16)
            sf[j][:, hh] = state.reshape(GROUP, PIECE, HEAD_DIM)
        spread(sf[j], srf[j], 4, state_sem.at[0, j])

    def backward_state(j):
        for hh, h in enumerate(BACK_SPANS[j]):
            state = tn(rows_of(QUERY, h) * heads[...], gr[h]).astype(BF16)
            sb[j][:, hh] = state.reshape(GROUP, PIECE, HEAD_DIM)
        spread(sb[j], srb[j], 7, state_sem.at[3, j])

    def last_of(zz, gg):
        return seg_all[gg, zz, 0:1, :]

    def first_of(zz, gg):
        return seg_all[gg, zz, 1:2, :]

    def flag(one, two):
        return jnp.where(one == two, 1.0, 0.0)

    def forward_flags():
        z1 = jnp.maximum(z - 1, 0)
        z2 = jnp.maximum(z - 2, 0)
        edge = last_of(z1, GROUP - 1)
        links = [flag(last_of(z, 0), edge)]
        for i in range(1, GROUP):
            links.append(flag(last_of(z, i), last_of(z, i - 1)))
        from_one = jnp.where(z >= 1, 1.0, 0.0)
        from_two = jnp.where(z >= 2, 1.0, 0.0) * flag(last_of(z2, GROUP - 1), edge)
        return links, from_one, from_two

    def backward_flags():
        z1 = jnp.minimum(z + 1, LINES - 1)
        z2 = jnp.minimum(z + 2, LINES - 1)
        edge = first_of(z1, 0)
        links = [flag(first_of(z, i), first_of(z, i + 1)) for i in range(GROUP - 1)]
        links.append(flag(first_of(z, GROUP - 1), edge))
        from_one = jnp.where(z <= LINES - 2, 1.0, 0.0)
        from_two = jnp.where(z <= LINES - 3, 1.0, 0.0) * flag(first_of(z2, 0), edge)
        return links, from_one, from_two

    def line_total(landed, mine_r, far, steps, links, stage, sem, direction):
        run = landed[steps[0]].astype(F32)
        for i in steps[1:]:
            run = landed[i].astype(F32) + links[i] * run
        mine_r[...] = run.astype(BF16)
        for n in (1, 0):
            zt = lax.rem(z + LINES + direction * (n + 1), LINES)
            send(mine_r, far.at[n], stage, sem, ctx_of(zt, g), y)

    def line_carry(landed, far, steps, flags, out, back, stage, far_sem, back_sem):
        links, from_one, from_two = flags
        took(far, far_sem)
        run = from_one * far[0].astype(F32) + from_two * far[1].astype(F32)
        out[steps[0]] = run.astype(BF16)
        for n in range(GROUP - 1):
            i = steps[n]
            run = landed[i].astype(F32) + links[i] * run
            out[steps[n + 1]] = run.astype(BF16)
        spread(out, back, stage, back_sem)

    up = tuple(range(GROUP))
    down = tuple(reversed(range(GROUP)))
    flags = {}

    def meet():
        gain_copy.wait()
        for h in range(OWN_HEADS):
            gain_rows[h] = gain[columns(h)].astype(F32).reshape(1, HEAD_DIM)
        took(seg_all.at[0 : GROUP - 1], small_sem.at[1])
        flags["ahead"] = forward_flags()
        flags["back"] = backward_flags()
        before = jnp.maximum(me - 1, 0)
        after = jnp.minimum(me + 1, LINES * GROUP - 1)
        here = jnp.broadcast_to(seg[...].astype(F32), (ROWS, ROWS)).T
        resume[...] = jnp.where(here == last_of(lax.div(before, GROUP), lax.rem(before, GROUP)), 1.0, 0.0)
        reaches[...] = jnp.where(here == first_of(lax.div(after, GROUP), lax.rem(after, GROUP)), 1.0, 0.0)

    def f_total(j):
        if not flags:
            meet()
        took(srf[j].at[0 : GROUP - 1], state_sem.at[0, j])
        line_total(srf[j], rf[j], zrf[j], up, flags["ahead"][0], 5, state_sem.at[1, j], 1)

    def f_carry(j):
        line_carry(
            srf[j], zrf[j], up, flags["ahead"], csf[j], crf[j], 6, state_sem.at[1, j], state_sem.at[2, j]
        )

    def b_total(j):
        took(srb[j].at[0 : GROUP - 1], state_sem.at[3, j])
        line_total(srb[j], rb[j], zrb[j], down, flags["back"][0], 8, state_sem.at[4, j], -1)

    def b_carry(j):
        line_carry(
            srb[j], zrb[j], down, flags["back"], csb[j], crb[j], 9, state_sem.at[4, j], state_sem.at[5, j]
        )

    def carried(ref, hh):
        return ref[:, hh].reshape(HEAD_DIM, HEAD_DIM)

    def weigh(j):
        for h in AHEAD_SPANS[j]:
            qh, kh = rows_of(QUERY, h), rows_of(KEY, h)
            weights = (nt(qh, kh) * vis[...]).astype(BF16)
            wt[h] = (nt(kh, qh) * vist[...]).astype(BF16)
            kg_part[h] = nn(weights, rows_of(VALUE, h))

    sums = []

    def attend(j):
        if not sums:
            ng_copy.wait()
        took(crf[j].at[0 : GROUP - 1], state_sem.at[2, j])
        squares, inner = 0.0, 0.0
        for hh, h in enumerate(AHEAD_SPANS[j]):
            out = kg_part[h] + resume[...] * nn(rows_of(QUERY, h), carried(crf[j], hh))
            out = out.astype(BF16)
            att[h] = out
            out = out.astype(F32)
            scaled = ng[:, columns(h)].astype(F32) * gain_rows[h]
            squares = squares + out * out
            inner = inner + scaled * out
        sums.append((squares, inner))

    work = dict(
        first_hop=first_hop, second_hop=second_hop, forward_state=forward_state,
        f_total=f_total, f_carry=f_carry, weigh=weigh, attend=attend,
    )
    for name, n in timeline():
        work[name](n)

    squares = sum(one for one, _ in sums)
    inner = sum(two for _, two in sums)
    sq_send[0:1, :] = jnp.sum(squares.T, axis=0, keepdims=True)
    sq_send[1:2, :] = jnp.sum(inner.T, axis=0, keepdims=True)
    for dy in (2, 1, 3):
        send(sq_send, sq_recv.at[y], 10, small_sem.at[2], me, lax.rem(y + dy, HEAD_PEERS))
    sq_recv[y] = sq_send[...]
    took(sq_recv.at[0 : HEAD_PEERS - 1], small_sem.at[2])
    total = (sq_recv[0] + sq_recv[1]) + (sq_recv[2] + sq_recv[3])
    width = HEADS * HEAD_DIM
    inverse = lax.rsqrt(total[0:1, :] / width + 1e-05)
    projection = inverse * total[1:2, :] / width
    inverse = jnp.broadcast_to(inverse, (ROWS, ROWS)).T
    projection = jnp.broadcast_to(projection, (ROWS, ROWS)).T

    for j, span in enumerate(BACK_SPANS):
        for h in span:
            scaled = ng[:, columns(h)].astype(F32) * gain_rows[h]
            normal = att[h].astype(F32) * inverse
            gr[h] = (inverse * (scaled - normal * projection)).astype(BF16)
        backward_state(j)

    def norm(h):
        normal = att[h].astype(F32) * inverse
        o_n[:, columns(h)] = (normal * gain_rows[h]).astype(BF16)

    def partial(h):
        j, hh = PLACE[h]
        qh, kh, vh, gh = rows_of(QUERY, h), rows_of(KEY, h), rows_of(VALUE, h), gr[h]
        grads = (nt(gh, vh) * vis[...]).astype(BF16)
        grads_t = (nt(vh, gh) * vist[...]).astype(BF16)
        query = nn(grads, kh) + resume[...] * nt(gh, carried(crf[j], hh))
        o_q[:, columns(h)] = query.astype(BF16)
        kg_part[h] = nn(grads_t, qh)
        vg_part[h] = nn(wt[h], gh)

    def finish(j):
        took(crb[j].at[0 : GROUP - 1], state_sem.at[5, j])
        for hh, h in enumerate(BACK_SPANS[j]):
            back = carried(crb[j], hh)
            key = kg_part[h] + reaches[...] * nt(rows_of(VALUE, h), back)
            o_k[:, columns(h)] = key.astype(BF16)
            value = vg_part[h] + reaches[...] * nn(rows_of(KEY, h), back)
            o_v[:, columns(h)] = value.astype(BF16)

    for h in range(OWN_HEADS):
        norm(h)
    for h in range(OWN_HEADS - 2):
        partial(h)
    for j in range(len(BACK)):
        b_total(j)
    for h in range(OWN_HEADS - 2, OWN_HEADS):
        partial(h)
    for j in range(len(BACK)):
        b_carry(j)
    for j in range(len(BACK)):
        finish(j)

    def left(ref, stage):
        pltpu.make_async_copy(ref, ref, send_sem.at[stage]).wait()

    left(seg_line.at[0 : LINES - 1], 1)
    left(seg_all.at[0 : GROUP - 1], 3)
    left(sq_recv.at[0 : HEAD_PEERS - 1], 10)
    for j in range(len(AHEAD)):
        left(a[j].at[:, 0 : ROWS - BAND], 0)
        left(c[j].at[:, 0 : ROWS - BAND], 2)
        left(sf[j].at[0 : GROUP - 1], 4)
        left(zrf[j], 5)
        left(csf[j].at[0 : GROUP - 1], 6)
    for j in range(len(BACK)):
        left(sb[j].at[0 : GROUP - 1], 7)
        left(zrb[j], 8)
        left(csb[j].at[0 : GROUP - 1], 9)


def deliver(n_in, q_in, k_in, v_in, n_out, q_out, k_out, v_out, sem):
    copies = []
    for i, (src, dst) in enumerate(((n_in, n_out), (q_in, q_out), (k_in, k_out), (v_in, v_out))):
        copy = pltpu.make_async_copy(src, dst, sem.at[i])
        copy.start()
        copies.append(copy)
    for copy in copies:
        copy.wait()


def shards(queries, keys, values, normed_grad, gain, segment, plan):
    vm = pltpu.VMEM

    def per(chunks, shape):
        return [vm(shape(n), BF16) for n in chunks]

    parcels = per(AHEAD, lambda n: (3, ROWS, n * HEAD_DIM))
    square = vm((ROWS, ROWS), F32)
    square_b = vm((ROWS, ROWS), BF16)
    by_head = vm((OWN_HEADS, ROWS, HEAD_DIM), BF16)
    by_head_f = vm((OWN_HEADS, ROWS, HEAD_DIM), F32)

    def state_set(chunks):
        states = per(chunks, lambda n: (GROUP, n, PIECE, HEAD_DIM))
        return [
            states, states, per(chunks, lambda n: (n, PIECE, HEAD_DIM)),
            per(chunks, lambda n: (2, n, PIECE, HEAD_DIM)), states, states,
        ]

    out = vm((ROWS, OWN_HEADS * HEAD_DIM), BF16)
    inputs = (
        queries, keys, values, normed_grad,
        gain, segment.reshape(1, -1), plan.reshape(LINES * GROUP, ROWS),
    )
    results = pl.pallas_call(
        kernel,
        out_shape=(out, out, out, out),
        in_specs=[pl.BlockSpec(memory_space=pltpu.HBM)] * 7,
        out_specs=[pl.BlockSpec(memory_space=pltpu.VMEM)] * 4,
        scratch_shapes=[
            parcels, parcels, parcels, parcels, parcels, parcels,
            vm((ROWS, OWN_HEADS * HEAD_DIM), BF16), vm((OWN_HEADS * HEAD_DIM,), BF16),
            vm((OWN_HEADS, 1, HEAD_DIM), F32),
            vm((1, ROWS), jnp.int32), vm((LINES * GROUP, ROWS), jnp.int32),
            vm((LINES, 2, ROWS), F32), vm((GROUP, LINES, 2, ROWS), F32),
            square_b, square_b, square, square, square_b, square_b, square, square,
            *state_set(AHEAD), *state_set(BACK),
            by_head, by_head, by_head, vm((8, ROWS), F32), vm((HEAD_PEERS, 8, ROWS), F32),
            by_head_f, by_head_f,
            pltpu.SemaphoreType.DMA((len(PARCELS) + 4,)),
            pltpu.SemaphoreType.DMA((11,)),
            pltpu.SemaphoreType.DMA((2, len(PARCELS))),
            pltpu.SemaphoreType.DMA((6, max(len(AHEAD), len(BACK)))),
            pltpu.SemaphoreType.DMA((3,)),
        ],
        compiler_params=pltpu.CompilerParams(
            collective_id=0, has_side_effects=True, vmem_limit_bytes=40 << 20
        ),
    )(*(pltpu.with_memory_space_constraint(t, pltpu.HBM) for t in inputs))
    final = jax.ShapeDtypeStruct(queries.shape, BF16)
    return tuple(pl.pallas_call(
        deliver,
        out_shape=(final, final, final, final),
        in_specs=[pl.BlockSpec(memory_space=pltpu.VMEM)] * 4,
        out_specs=[pl.BlockSpec(memory_space=pltpu.HBM)] * 4,
        scratch_shapes=[pltpu.SemaphoreType.DMA((4,))],
    )(*(pltpu.with_memory_space_constraint(t, pltpu.VMEM) for t in results)))


def solution(mesh):
    both = P("ctx", "head")
    return jax.shard_map(
        shards,
        mesh=mesh,
        in_specs=(both, both, both, both, P("head"), P("ctx"), P()),
        out_specs=(both, both, both, both),
        check_vma=False,
    )
```

```python
import jax
import jax.numpy as jnp
from jax import lax
from jax.experimental import pallas as pl
from jax.experimental.pallas import tpu as pltpu
from jax.sharding import PartitionSpec as P

HEADS = 48
HEAD_DIM = 128
ROWS = 128
LINES = 8
GROUP = 8
OWN_HEADS = 12
AHEAD = (4, 3, 3, 2)
BACK = (2, 4, 4, 2)
BAND = ROWS // LINES
WINDOW = 2.0
PIECE = HEAD_DIM // GROUP
HEAD_PEERS = 4
MESH = pl.DeviceIdType.MESH
F32 = jnp.float32
BF16 = jnp.bfloat16
Z_ORDER = (4, 3, 5, 2, 6, 1, 7)
G_ORDER = (4, 3, 5, 2, 6, 1, 7)

KEY, VALUE, QUERY = 0, 1, 2
PARCELS = [(t, j) for j in range(len(AHEAD)) for t in (KEY, VALUE)]
PARCELS += [(QUERY, j) for j in range(len(AHEAD))]


def spans(chunks):
    firsts = [sum(chunks[:j]) for j in range(len(chunks))]
    return [range(f, f + n) for f, n in zip(firsts, chunks)]


AHEAD_SPANS = spans(AHEAD)
BACK_SPANS = spans(BACK)
PLACE = {h: (j, h - span[0]) for j, span in enumerate(AHEAD_SPANS) for h in span}


def timeline():
    wire_z, late_z, wire_x, late_x, wire_line, late_line = 0.7, 4.0, 0.36, 3.2, 0.26, 3.0
    starts, clock = [], 0.0
    for t, j in PARCELS:
        starts.append(clock)
        clock += wire_z * AHEAD[j]
    totals = [99.0 + j for j in range(len(AHEAD))]
    for _ in range(4):
        queue = [(start - WINDOW, wire_z * AHEAD[j], ("p", p)) for p, ((t, j), start) in enumerate(zip(PARCELS, starts))]
        queue += [(when, wire_line * AHEAD[j], ("r", j)) for j, when in enumerate(totals)]
        clock, there = 0.0, {}
        for issue, takes, what in sorted(queue):
            clock = max(clock, issue) + takes
            there[what] = clock
        second = {
            parcel: there["p", p] + late_z + 4.4 + 0.1 * AHEAD[parcel[1]]
            for p, parcel in enumerate(PARCELS)
        }
        totals = [second[VALUE, j] + 0.02 + late_x + 0.3 * n for j, n in enumerate(AHEAD)]
    events = []
    for p, parcel in enumerate(PARCELS):
        if starts[p] > WINDOW:
            events.append((starts[p] - WINDOW, "depart", p))
        events.append((there["p", p] + late_z, "first_hop", p))
        events.append((second[parcel], "second_hop", p))
    for j, n in enumerate(AHEAD):
        carry = there["r", j] + late_line
        events.append((second[VALUE, j] + 0.01, "forward_state", j))
        events.append((totals[j], "f_total", j))
        events.append((carry, "f_carry", j))
        events.append((second[QUERY, j] + 0.01, "weigh", j))
        events.append((max(carry + late_x + wire_x * n, second[QUERY, j] + 0.02), "attend", j))
    return [event[1:] for event in sorted(events)]


def nn(a, b):
    return lax.dot_general(a, b, (((1,), (0,)), ((), ())), preferred_element_type=F32)


def nt(a, b):
    return lax.dot_general(a, b, (((1,), (1,)), ((), ())), preferred_element_type=F32)


def tn(a, b):
    return lax.dot_general(a, b, (((0,), (0,)), ((), ())), preferred_element_type=F32)


def iota(dim):
    return lax.broadcasted_iota(jnp.int32, (ROWS, ROWS), dim)


def kernel(
    q_hbm, k_hbm, v_hbm, ng_hbm, gain_hbm, seg_hbm, plan_hbm,
    o_n, o_q, o_k, o_v,
    x, a, b, c, d, seq, ng, gain, gain_rows, seg, plan,
    seg_line, seg_all, mid, settle, vis, vist, tails, heads, resume, reaches,
    sf, srf, rf, zrf, csf, crf, sb, srb, rb, zrb, csb, crb,
    att, gr, wt, sq_send, sq_recv, kg_part, vg_part,
    load_sem, send_sem, hop_sem, state_sem, small_sem,
):
    me = lax.axis_index("ctx")
    y = lax.axis_index("head")
    z = lax.div(me, GROUP)
    g = lax.rem(me, GROUP)

    def z_peer(dz):
        return lax.rem(z + dz, LINES)

    def g_peer(dg):
        return lax.rem(g + dg, GROUP)

    def ctx_of(zz, gg):
        return zz * GROUP + gg

    def band(i):
        return pl.ds(pl.multiple_of(i * BAND, BAND), BAND)

    def send(src, dst, stage, sem, ctx_to, head_to):
        pltpu.make_async_remote_copy(
            src_ref=src, dst_ref=dst, send_sem=send_sem.at[stage], recv_sem=sem,
            device_id=(ctx_to, head_to), device_id_type=MESH,
        ).start()

    def took(ref, sem):
        pltpu.make_async_copy(ref, ref, sem).wait()

    barrier = pltpu.get_barrier_semaphore()
    for dz in Z_ORDER:
        pl.semaphore_signal(barrier, inc=1, device_id=(ctx_of(z_peer(dz), g), y), device_id_type=MESH)
    for dg in G_ORDER:
        pl.semaphore_signal(barrier, inc=1, device_id=(ctx_of(z, g_peer(dg)), y), device_id_type=MESH)
    for dy in range(1, HEAD_PEERS):
        pl.semaphore_signal(
            barrier, inc=1, device_id=(me, lax.rem(y + dy, HEAD_PEERS)), device_id_type=MESH
        )

    plan_copy = pltpu.make_async_copy(plan_hbm, plan, load_sem.at[len(PARCELS)])
    plan_copy.start()
    seg_copy = pltpu.make_async_copy(seg_hbm, seg, load_sem.at[len(PARCELS) + 1])
    seg_copy.start()
    loads = []
    for p, (t, j) in enumerate(PARCELS):
        span = AHEAD_SPANS[j]
        cols = slice(span.start * HEAD_DIM, span.stop * HEAD_DIM)
        copy = pltpu.make_async_copy((k_hbm, v_hbm, q_hbm)[t].at[:, cols], x[j].at[t], load_sem.at[p])
        copy.start()
        loads.append(copy)
    gain_copy = pltpu.make_async_copy(gain_hbm, gain, load_sem.at[len(PARCELS) + 2])
    gain_copy.start()
    ng_copy = pltpu.make_async_copy(ng_hbm, ng, load_sem.at[len(PARCELS) + 3])
    ng_copy.start()

    plan_copy.wait()
    rows_i = iota(0)
    cols_i = iota(1)
    own_plan = plan[pl.ds(me, 1), :]
    slot_of = 2 * lax.shift_right_logical(own_plan, 7) + (cols_i[0:1, :] & 1)
    leave = (rows_i == slot_of).astype(F32).astype(BF16)

    def sort(p):
        t, j = PARCELS[p]
        loads[p].wait()
        a[j][t] = nn(leave, x[j][t]).astype(BF16)

    def depart(p):
        t, j = PARCELS[p]
        for dz in Z_ORDER:
            zt = z_peer(dz)
            send(a[j].at[t, band(zt)], b[j].at[t, band(z)], 0, hop_sem.at[0, p], ctx_of(zt, g), y)
        b[j][t, band(z), :] = a[j][t, band(z), :]

    seg_copy.wait()
    seg_f = seg[...].astype(F32)
    last_here = jnp.broadcast_to(seg_f[:, ROWS - 1 : ROWS], (1, ROWS))
    first_here = jnp.broadcast_to(seg_f[:, 0:1], (1, ROWS))
    seg_line[z, 0:1, :] = last_here
    seg_line[z, 1:2, :] = first_here
    sort(0)

    pl.semaphore_wait(barrier, LINES - 1 + GROUP - 1 + HEAD_PEERS - 1)

    steps = timeline()
    for dz in Z_ORDER:
        send(seg_line.at[z], seg_line.at[z], 1, small_sem.at[0], ctx_of(z_peer(dz), g), y)
    depart(0)
    for p, (t, j) in enumerate(PARCELS):
        if p > 0:
            sort(p)
            if ("depart", p) not in steps:
                depart(p)

    seg_lanes = jnp.broadcast_to(seg_f, (ROWS, ROWS))
    seg_rows = seg_lanes.T
    same = seg_lanes == seg_rows
    vis[...] = jnp.where(same & (rows_i >= cols_i), 1.0, 0.0)
    vist[...] = jnp.where(same & (cols_i >= rows_i), 1.0, 0.0)
    tails[...] = jnp.where(seg_rows == last_here, 1.0, 0.0).astype(BF16)
    heads[...] = jnp.where(seg_rows == first_here, 1.0, 0.0).astype(BF16)

    source = ((rows_i & 15) >> 1) * BAND + (rows_i >> 4) * 2 + (rows_i & 1)
    mid[...] = (cols_i == source).astype(F32).astype(BF16)
    plan_all = plan[...]
    lanes = lax.broadcasted_iota(jnp.int32, (LINES * GROUP, ROWS), 1)
    mine = (lax.shift_right_logical(plan_all, 7) == me) & ((lanes & 1) == 0)
    start = jnp.sum(jnp.where(mine, (plan_all & 127).astype(F32), 0.0), axis=1, keepdims=True)
    start = jnp.broadcast_to(start, (LINES * GROUP, ROWS)).astype(BF16)
    pick_rows = lax.broadcasted_iota(jnp.int32, (ROWS, LINES * GROUP), 0)
    pick_cols = lax.broadcasted_iota(jnp.int32, (ROWS, LINES * GROUP), 1)
    pick = (pick_cols == ((pick_rows & 15) >> 1) * GROUP + (pick_rows >> 4)).astype(F32).astype(BF16)
    place = nn(pick, start) + (rows_i & 1).astype(F32)
    settle[...] = jnp.where(cols_i.astype(F32) == place, 1.0, 0.0).T.astype(BF16)

    def first_hop(p):
        t, j = PARCELS[p]
        took(b[j].at[t, 0 : ROWS - BAND], hop_sem.at[0, p])
        c[j][t] = nn(mid[...], b[j][t]).astype(BF16)
        for dg in G_ORDER:
            gt = g_peer(dg)
            send(c[j].at[t, band(gt)], d[j].at[t, band(g)], 2, hop_sem.at[1, p], ctx_of(z, gt), y)
        d[j][t, band(g), :] = c[j][t, band(g), :]
        if p == 0:
            took(seg_line.at[0 : LINES - 1], small_sem.at[0])
            seg_all[g] = seg_line[...]
            for dg in G_ORDER:
                send(seg_line, seg_all.at[g], 3, small_sem.at[1], ctx_of(z, g_peer(dg)), y)

    def second_hop(p):
        t, j = PARCELS[p]
        took(d[j].at[t, 0 : ROWS - BAND], hop_sem.at[1, p])
        seq[j][t] = nn(settle[...], d[j][t]).astype(BF16)

    def rows_of(t, h):
        j, hh = PLACE[h]
        return seq[j][t, :, HEAD_DIM * hh : HEAD_DIM * (hh + 1)]

    def columns(h):
        return slice(HEAD_DIM * h, HEAD_DIM * (h + 1))

    def spread(local, landed, stage, sem):
        for dg in G_ORDER:
            gt = g_peer(dg)
            send(local.at[gt], landed.at[g], stage, sem, ctx_of(z, gt), y)
        landed[g] = local[g]

    def forward_state(j):
        for hh, h in enumerate(AHEAD_SPANS[j]):
            state = tn(rows_of(KEY, h) * tails[...], rows_of(VALUE, h)).astype(BF16)
            sf[j][:, hh] = state.reshape(GROUP, PIECE, HEAD_DIM)
        spread(sf[j], srf[j], 4, state_sem.at[0, j])

    def backward_state(j):
        for hh, h in enumerate(BACK_SPANS[j]):
            state = tn(rows_of(QUERY, h) * heads[...], gr[h]).astype(BF16)
            sb[j][:, hh] = state.reshape(GROUP, PIECE, HEAD_DIM)
        spread(sb[j], srb[j], 7, state_sem.at[3, j])

    def last_of(zz, gg):
        return seg_all[gg, zz, 0:1, :]

    def first_of(zz, gg):
        return seg_all[gg, zz, 1:2, :]

    def flag(one, two):
        return jnp.where(one == two, 1.0, 0.0)

    def forward_flags():
        z1 = jnp.maximum(z - 1, 0)
        z2 = jnp.maximum(z - 2, 0)
        edge = last_of(z1, GROUP - 1)
        links = [flag(last_of(z, 0), edge)]
        for i in range(1, GROUP):
            links.append(flag(last_of(z, i), last_of(z, i - 1)))
        from_one = jnp.where(z >= 1, 1.0, 0.0)
        from_two = jnp.where(z >= 2, 1.0, 0.0) * flag(last_of(z2, GROUP - 1), edge)
        return links, from_one, from_two

    def backward_flags():
        z1 = jnp.minimum(z + 1, LINES - 1)
        z2 = jnp.minimum(z + 2, LINES - 1)
        edge = first_of(z1, 0)
        links = [flag(first_of(z, i), first_of(z, i + 1)) for i in range(GROUP - 1)]
        links.append(flag(first_of(z, GROUP - 1), edge))
        from_one = jnp.where(z <= LINES - 2, 1.0, 0.0)
        from_two = jnp.where(z <= LINES - 3, 1.0, 0.0) * flag(first_of(z2, 0), edge)
        return links, from_one, from_two

    def line_total(landed, mine_r, far, steps, links, stage, sem, direction):
        run = landed[steps[0]].astype(F32)
        for i in steps[1:]:
            run = landed[i].astype(F32) + links[i] * run
        mine_r[...] = run.astype(BF16)
        for n in (1, 0):
            zt = lax.rem(z + LINES + direction * (n + 1), LINES)
            send(mine_r, far.at[n], stage, sem, ctx_of(zt, g), y)

    def line_carry(landed, far, steps, flags, out, back, stage, far_sem, back_sem):
        links, from_one, from_two = flags
        took(far, far_sem)
        run = from_one * far[0].astype(F32) + from_two * far[1].astype(F32)
        out[steps[0]] = run.astype(BF16)
        for n in range(GROUP - 1):
            i = steps[n]
            run = landed[i].astype(F32) + links[i] * run
            out[steps[n + 1]] = run.astype(BF16)
        spread(out, back, stage, back_sem)

    up = tuple(range(GROUP))
    down = tuple(reversed(range(GROUP)))
    flags = {}

    def meet():
        gain_copy.wait()
        for h in range(OWN_HEADS):
            gain_rows[h] = gain[columns(h)].astype(F32).reshape(1, HEAD_DIM)
        took(seg_all.at[0 : GROUP - 1], small_sem.at[1])
        flags["ahead"] = forward_flags()
        flags["back"] = backward_flags()
        before = jnp.maximum(me - 1, 0)
        after = jnp.minimum(me + 1, LINES * GROUP - 1)
        here = jnp.broadcast_to(seg[...].astype(F32), (ROWS, ROWS)).T
        resume[...] = jnp.where(here == last_of(lax.div(before, GROUP), lax.rem(before, GROUP)), 1.0, 0.0)
        reaches[...] = jnp.where(here == first_of(lax.div(after, GROUP), lax.rem(after, GROUP)), 1.0, 0.0)

    def f_total(j):
        if not flags:
            meet()
        took(srf[j].at[0 : GROUP - 1], state_sem.at[0, j])
        line_total(srf[j], rf[j], zrf[j], up, flags["ahead"][0], 5, state_sem.at[1, j], 1)

    def f_carry(j):
        line_carry(
            srf[j], zrf[j], up, flags["ahead"], csf[j], crf[j], 6, state_sem.at[1, j], state_sem.at[2, j]
        )

    def b_total(j):
        took(srb[j].at[0 : GROUP - 1], state_sem.at[3, j])
        line_total(srb[j], rb[j], zrb[j], down, flags["back"][0], 8, state_sem.at[4, j], -1)

    def b_carry(j):
        line_carry(
            srb[j], zrb[j], down, flags["back"], csb[j], crb[j], 9, state_sem.at[4, j], state_sem.at[5, j]
        )

    def carried(ref, hh):
        return ref[:, hh].reshape(HEAD_DIM, HEAD_DIM)

    def weigh(j):
        for h in AHEAD_SPANS[j]:
            qh, kh = rows_of(QUERY, h), rows_of(KEY, h)
            weights = (nt(qh, kh) * vis[...]).astype(BF16)
            wt[h] = (nt(kh, qh) * vist[...]).astype(BF16)
            kg_part[h] = nn(weights, rows_of(VALUE, h))

    sums = []

    def attend(j):
        if not sums:
            ng_copy.wait()
        took(crf[j].at[0 : GROUP - 1], state_sem.at[2, j])
        squares, inner = 0.0, 0.0
        for hh, h in enumerate(AHEAD_SPANS[j]):
            out = kg_part[h] + resume[...] * nn(rows_of(QUERY, h), carried(crf[j], hh))
            out = out.astype(BF16)
            att[h] = out
            out = out.astype(F32)
            scaled = ng[:, columns(h)].astype(F32) * gain_rows[h]
            squares = squares + out * out
            inner = inner + scaled * out
        sums.append((squares, inner))

    work = dict(
        depart=depart, first_hop=first_hop, second_hop=second_hop, forward_state=forward_state,
        f_total=f_total, f_carry=f_carry, weigh=weigh, attend=attend,
    )
    for name, n in steps:
        work[name](n)

    squares = sum(one for one, _ in sums)
    inner = sum(two for _, two in sums)
    sq_send[0:1, :] = jnp.sum(squares.T, axis=0, keepdims=True)
    sq_send[1:2, :] = jnp.sum(inner.T, axis=0, keepdims=True)
    for dy in (2, 1, 3):
        send(sq_send, sq_recv.at[y], 10, small_sem.at[2], me, lax.rem(y + dy, HEAD_PEERS))
    sq_recv[y] = sq_send[...]
    took(sq_recv.at[0 : HEAD_PEERS - 1], small_sem.at[2])
    total = (sq_recv[0] + sq_recv[1]) + (sq_recv[2] + sq_recv[3])
    width = HEADS * HEAD_DIM
    inverse = lax.rsqrt(total[0:1, :] / width + 1e-05)
    projection = inverse * total[1:2, :] / width
    inverse = jnp.broadcast_to(inverse, (ROWS, ROWS)).T
    projection = jnp.broadcast_to(projection, (ROWS, ROWS)).T

    for j, span in enumerate(BACK_SPANS):
        for h in span:
            scaled = ng[:, columns(h)].astype(F32) * gain_rows[h]
            normal = att[h].astype(F32) * inverse
            gr[h] = (inverse * (scaled - normal * projection)).astype(BF16)
        backward_state(j)

    def norm(h):
        normal = att[h].astype(F32) * inverse
        o_n[:, columns(h)] = (normal * gain_rows[h]).astype(BF16)

    def partial(h):
        j, hh = PLACE[h]
        qh, kh, vh, gh = rows_of(QUERY, h), rows_of(KEY, h), rows_of(VALUE, h), gr[h]
        grads = (nt(gh, vh) * vis[...]).astype(BF16)
        grads_t = (nt(vh, gh) * vist[...]).astype(BF16)
        query = nn(grads, kh) + resume[...] * nt(gh, carried(crf[j], hh))
        o_q[:, columns(h)] = query.astype(BF16)
        kg_part[h] = nn(grads_t, qh)
        vg_part[h] = nn(wt[h], gh)

    def finish(j):
        took(crb[j].at[0 : GROUP - 1], state_sem.at[5, j])
        for hh, h in enumerate(BACK_SPANS[j]):
            back = carried(crb[j], hh)
            key = kg_part[h] + reaches[...] * nt(rows_of(VALUE, h), back)
            o_k[:, columns(h)] = key.astype(BF16)
            value = vg_part[h] + reaches[...] * nn(rows_of(KEY, h), back)
            o_v[:, columns(h)] = value.astype(BF16)

    for h in range(OWN_HEADS):
        norm(h)
    for h in range(OWN_HEADS - 2):
        partial(h)
    for j in range(len(BACK)):
        b_total(j)
    for h in range(OWN_HEADS - 2, OWN_HEADS):
        partial(h)
    for j in range(len(BACK)):
        b_carry(j)
    for j in range(len(BACK)):
        finish(j)

    def left(ref, stage):
        pltpu.make_async_copy(ref, ref, send_sem.at[stage]).wait()

    left(seg_line.at[0 : LINES - 1], 1)
    left(seg_all.at[0 : GROUP - 1], 3)
    left(sq_recv.at[0 : HEAD_PEERS - 1], 10)
    for j in range(len(AHEAD)):
        left(a[j].at[:, 0 : ROWS - BAND], 0)
        left(c[j].at[:, 0 : ROWS - BAND], 2)
        left(sf[j].at[0 : GROUP - 1], 4)
        left(zrf[j], 5)
        left(csf[j].at[0 : GROUP - 1], 6)
    for j in range(len(BACK)):
        left(sb[j].at[0 : GROUP - 1], 7)
        left(zrb[j], 8)
        left(csb[j].at[0 : GROUP - 1], 9)


def deliver(n_in, q_in, k_in, v_in, n_out, q_out, k_out, v_out, sem):
    copies = []
    for i, (src, dst) in enumerate(((n_in, n_out), (q_in, q_out), (k_in, k_out), (v_in, v_out))):
        copy = pltpu.make_async_copy(src, dst, sem.at[i])
        copy.start()
        copies.append(copy)
    for copy in copies:
        copy.wait()


def shards(queries, keys, values, normed_grad, gain, segment, plan):
    vm = pltpu.VMEM

    def per(chunks, shape):
        return [vm(shape(n), BF16) for n in chunks]

    parcels = per(AHEAD, lambda n: (3, ROWS, n * HEAD_DIM))
    square = vm((ROWS, ROWS), F32)
    square_b = vm((ROWS, ROWS), BF16)
    by_head = vm((OWN_HEADS, ROWS, HEAD_DIM), BF16)
    by_head_f = vm((OWN_HEADS, ROWS, HEAD_DIM), F32)

    def state_set(chunks):
        states = per(chunks, lambda n: (GROUP, n, PIECE, HEAD_DIM))
        return [
            states, states, per(chunks, lambda n: (n, PIECE, HEAD_DIM)),
            per(chunks, lambda n: (2, n, PIECE, HEAD_DIM)), states, states,
        ]

    out = vm((ROWS, OWN_HEADS * HEAD_DIM), BF16)
    inputs = (
        queries, keys, values, normed_grad,
        gain, segment.reshape(1, -1), plan.reshape(LINES * GROUP, ROWS),
    )
    results = pl.pallas_call(
        kernel,
        out_shape=(out, out, out, out),
        in_specs=[pl.BlockSpec(memory_space=pltpu.HBM)] * 7,
        out_specs=[pl.BlockSpec(memory_space=pltpu.VMEM)] * 4,
        scratch_shapes=[
            parcels, parcels, parcels, parcels, parcels, parcels,
            vm((ROWS, OWN_HEADS * HEAD_DIM), BF16), vm((OWN_HEADS * HEAD_DIM,), BF16),
            vm((OWN_HEADS, 1, HEAD_DIM), F32),
            vm((1, ROWS), jnp.int32), vm((LINES * GROUP, ROWS), jnp.int32),
            vm((LINES, 2, ROWS), F32), vm((GROUP, LINES, 2, ROWS), F32),
            square_b, square_b, square, square, square_b, square_b, square, square,
            *state_set(AHEAD), *state_set(BACK),
            by_head, by_head, by_head, vm((8, ROWS), F32), vm((HEAD_PEERS, 8, ROWS), F32),
            by_head_f, by_head_f,
            pltpu.SemaphoreType.DMA((len(PARCELS) + 4,)),
            pltpu.SemaphoreType.DMA((11,)),
            pltpu.SemaphoreType.DMA((2, len(PARCELS))),
            pltpu.SemaphoreType.DMA((6, max(len(AHEAD), len(BACK)))),
            pltpu.SemaphoreType.DMA((3,)),
        ],
        compiler_params=pltpu.CompilerParams(
            collective_id=0, has_side_effects=True, vmem_limit_bytes=40 << 20
        ),
    )(*(pltpu.with_memory_space_constraint(t, pltpu.HBM) for t in inputs))
    final = jax.ShapeDtypeStruct(queries.shape, BF16)
    return tuple(pl.pallas_call(
        deliver,
        out_shape=(final, final, final, final),
        in_specs=[pl.BlockSpec(memory_space=pltpu.VMEM)] * 4,
        out_specs=[pl.BlockSpec(memory_space=pltpu.HBM)] * 4,
        scratch_shapes=[pltpu.SemaphoreType.DMA((4,))],
    )(*(pltpu.with_memory_space_constraint(t, pltpu.VMEM) for t in results)))


def solution(mesh):
    both = P("ctx", "head")
    return jax.shard_map(
        shards,
        mesh=mesh,
        in_specs=(both, both, both, both, P("head"), P("ctx"), P()),
        out_specs=(both, both, both, both),
        check_vma=False,
    )
```
